32 devices in a mesh: front: 8 (over z, x), rhs: 4 (over y, core).
Axes of the slice: x: 2, y: 2, z: 4, core: 2. Of those that a mesh axis runs over, the one named last changes fastest.
Arguments:
- signs: int32 [128, 512], P('rhs'), may hold values from -1 to 1, as said below
- sources: bfloat16 [512, 16384], P(None, 'front'), may hold values from -0.25 to 0.25
- dinv: float32 [64, 256, 256], P('front')
- u_fac: float32 [64, 256, 32], P('front')
- v_fac: float32 [64, 256, 32], P('front')
- ranks: int32 [64], P('front'), may hold values from 8 to 32
- dobs: bfloat16 [128, 16384], P('rhs', 'front'), may hold values from -6 to 6
- cellmap: int32 [16384], replicated, may hold values from 0 to 65535, as said below
Outputs:
- wavefield: float32 [128, 16384], P('rhs', 'front')
- adjoint_field: float32 [128, 16384], P('rhs', 'front')
- gradient: float32 [65536], P('front')
The draws below stay inside these ranges and needn't reach their ends.
Inputs may be any that keep to these rules, and one draw needn't show every extreme that they name: `signs`: each entry is -1 or 1. `cellmap`: model cell m belongs to owner m // 8192; among the cells k * 8 * 256 to (k + 1) * 8 * 256 - 1, for each k, at most 512 have one owner, and in every such block some owner has exactly 512.
All inputs are finite; a program needn't handle non-finite values.
Results may differ from the reference program's by a relative error of at most 0.0003.
Values sent between devices are 32-bit elements; how exact they have to be, the bound alone decides.
No kernel may reach another device: no remote copies, remote signals or barrier semaphores. Data moves between devices by JAX's collectives and lax.ppermute only.
A program may use at most 64 MiB of HBM per device.

```python
import math
import jax
import jax.numpy as jnp
from jax import lax

BS = 256
RMAX = 32
NSRC = 512
FB = 8
MC_DEV = 8192
NB = 64
CELLS = 16384
NRHS = 128
NM = 65536
CAP = 512
N_FRONT = 8


def draw_signs(key, part):
    return 2 * jax.random.randint(key, (NRHS, NSRC), 0, 2, dtype=jnp.int32) - 1


def spread_noise(key, shape, scale):
    return jax.random.normal(key, shape, jnp.float32) * scale


def chain_parts(key):
    first, second, third = jax.random.split(jax.random.fold_in(key, 61), 3)
    diagonal = jax.random.uniform(first, (NB, BS), jnp.float32, 0.6, 1.2)
    row_signs = (2 * jax.random.randint(second, (NB, BS), 0, 2, dtype=jnp.int32) - 1).astype(jnp.float32)
    column_keys = jax.random.split(third, NB)
    picks = jax.vmap(lambda one_key: jax.random.permutation(one_key, BS)[:RMAX])(column_keys).astype(jnp.int32)
    cell_ids = jnp.arange(BS, dtype=jnp.int32)
    common_bits = jnp.bitwise_and(cell_ids[None, :, None], picks[:, None, :])
    parity = jnp.zeros_like(common_bits)
    for level in range(BS.bit_length() - 1):
        parity = jnp.bitwise_xor(parity, jnp.bitwise_and(jnp.right_shift(common_bits, level), 1))
    hadamard = (1 - 2 * parity).astype(jnp.float32)
    left = row_signs[:, :, None] * hadamard * (1.0 / math.sqrt(BS))
    return (diagonal, left)


def draw_dinv(key, part):
    diagonal, left = chain_parts(key)
    identity = jnp.eye(BS, dtype=jnp.float32)
    offdiag = spread_noise(jax.random.fold_in(key, 11), (NB, BS, BS), 0.24 / math.sqrt(BS))
    return offdiag * (1.0 - identity) + identity * diagonal[:, None, :]


def draw_u_fac(key, part):
    diagonal, left = chain_parts(key)
    return left


def draw_v_fac(key, part):
    diagonal, left = chain_parts(key)
    keep = math.exp(-1.0 / NB)
    previous_left = jnp.roll(left, 1, axis=0)
    previous_diag = jnp.roll(diagonal, 1, axis=0)
    return keep * previous_left / previous_diag[:, :, None]


def draw_ranks(key, part):
    first, second, third = jax.random.split(jax.random.fold_in(key, 41), 3)
    values = jax.random.randint(first, (NB,), RMAX // 4, RMAX + 1, dtype=jnp.int32)
    top_place = jax.random.randint(second, (), 0, NB, dtype=jnp.int32)
    low_place = (top_place + 1 + jax.random.randint(third, (), 0, NB - 1, dtype=jnp.int32)) % NB
    values = values.at[top_place].set(RMAX)
    values = values.at[low_place].set(RMAX // 4)
    return values


def draw_cellmap(key, part):
    first, second, third = jax.random.split(jax.random.fold_in(key, 51), 3)
    rows = FB * BS
    base = jax.random.randint(first, (), 0, N_FRONT, dtype=jnp.int32)
    favored_all = (base + jnp.arange(N_FRONT, dtype=jnp.int32)) % N_FRONT

    def one_block(block_key, favored):
        pair_key, share_key, shuffle_key = jax.random.split(block_key, 3)
        order = jax.random.permutation(pair_key, N_FRONT).astype(jnp.int32)
        leading = order[0::2]
        trailing = order[1::2]
        shares = jax.random.randint(share_key, (N_FRONT // 2,), 0, CAP + 1, dtype=jnp.int32)
        shares = jnp.where(leading == favored, CAP, jnp.where(trailing == favored, 0, shares))
        counts = jnp.zeros((N_FRONT,), jnp.int32).at[leading].set(shares).at[trailing].set(CAP - shares)
        bounds = jnp.cumsum(counts)
        slot_ids = jnp.arange(rows, dtype=jnp.int32)
        owner_of_slot = jnp.sum((slot_ids[:, None] >= bounds[None, :]).astype(jnp.int32), axis=1)
        return jax.random.permutation(shuffle_key, owner_of_slot)
    owners = jax.vmap(one_block)(jax.random.split(second, N_FRONT), favored_all).reshape(CELLS).astype(jnp.int32)
    offsets = jax.random.randint(third, (CELLS,), 0, MC_DEV, dtype=jnp.int32)
    top_cell = jnp.argmax(owners).astype(jnp.int32)
    low_cell = jnp.argmin(owners).astype(jnp.int32)
    offsets = offsets.at[top_cell].set(MC_DEV - 1)
    offsets = offsets.at[low_cell].set(0)
    return owners * MC_DEV + offsets


def block_scale(own_key, extent, pieces, least, top_value):
    def one(axis_at, blocks):
        heights = jax.random.uniform(jax.random.fold_in(jax.random.fold_in(own_key, 6), axis_at), (blocks,), jnp.float32, least / len(pieces), top_value / len(pieces))
        return jnp.repeat(jnp.exp(heights), extent[axis_at] // blocks).reshape((-1,) + (1,) * (len(extent) - axis_at - 1))

    gain = one(*pieces[0])
    for cut in pieces[1:]:
        gain = gain * one(*cut)
    return gain


def noise(own_key, dims, width, most, pieces=(), held_as=jnp.bfloat16):
    gain = block_scale(own_key, dims, pieces, -0.22, 0.18) if pieces else 1.0
    result = jax.random.normal(own_key, dims, jnp.float32) * width * gain
    return jnp.minimum(jnp.maximum(result, -most), most).astype(held_as)


def setup_inputs(seed: int = 0) -> dict:
    key_of = jax.random.split(jax.random.key(seed), 9)
    signs = draw_signs(jax.random.fold_in(key_of[8], 71), 0)
    sources = noise(key_of[1], (NSRC, CELLS), NSRC ** -0.5, 0.25, ((1, 8),))
    dinv = draw_dinv(jax.random.fold_in(key_of[8], 71), 0)
    u_fac = draw_u_fac(jax.random.fold_in(key_of[8], 71), 0)
    v_fac = draw_v_fac(jax.random.fold_in(key_of[8], 71), 0)
    ranks = draw_ranks(jax.random.fold_in(key_of[8], 71), 0)
    dobs = noise(key_of[6], (NRHS, CELLS), 1.0, 6.0, ((0, 4), (1, 8)))
    cellmap = draw_cellmap(jax.random.fold_in(key_of[8], 71), 0)
    return {"signs": signs, "sources": sources, "dinv": dinv, "u_fac": u_fac, "v_fac": v_fac, "ranks": ranks, "dobs": dobs, "cellmap": cellmap}


HIGHEST = lax.Precision.HIGHEST


def forward_step(state, inputs):
    source, inverse, left, right_next = inputs
    field = jnp.dot(source - jnp.dot(state, left.T, precision=HIGHEST), inverse.T, precision=HIGHEST)
    return jnp.dot(field, right_next, precision=HIGHEST), field


def adjoint_step(state, inputs):
    source, inverse, left, right_next = inputs
    field = jnp.dot(source - jnp.dot(state, right_next.T, precision=HIGHEST), inverse, precision=HIGHEST)
    return jnp.dot(field, left, precision=HIGHEST), field


def reference(signs, sources, dinv, u_fac, v_fac, ranks, dobs, cellmap):
    encoded = jnp.dot(signs.astype(jnp.bfloat16), sources, preferred_element_type=jnp.float32)
    live = (jnp.arange(RMAX)[None, :] < ranks[:, None]).astype(jnp.float32)
    left_live = u_fac * live[:, None, :]
    right_live = v_fac * live[:, None, :]
    right_next = jnp.concatenate([right_live[1:], jnp.zeros((1, BS, RMAX), jnp.float32)], axis=0)
    source_blocks = encoded.reshape(NRHS, NB, BS).transpose(1, 0, 2)
    start = jnp.zeros((NRHS, RMAX), jnp.float32)
    ignored, wave = lax.scan(forward_step, start, (source_blocks, dinv, left_live, right_next))
    residual = wave - dobs.astype(jnp.float32).reshape(NRHS, NB, BS).transpose(1, 0, 2)
    ignored_back, adjoint = lax.scan(adjoint_step, start, (residual, dinv, left_live, right_next), reverse=True)
    image = (jnp.sum(wave * adjoint, axis=1) / NRHS).reshape(CELLS)
    gradient = jnp.zeros((NM,), jnp.float32).at[cellmap].add(image)
    wavefield = wave.transpose(1, 0, 2).reshape(NRHS, CELLS)
    adjoint_field = adjoint.transpose(1, 0, 2).reshape(NRHS, CELLS)
    return wavefield, adjoint_field, gradient
```

```python
import functools

import jax
import jax.numpy as jnp
from jax import lax
from jax.experimental import pallas as pl
from jax.experimental.pallas import tpu as pltpu
from jax.sharding import PartitionSpec as P

MC_DEV = 8192
LANES = 128
F32 = jnp.float32
BF16 = jnp.bfloat16
HIGH = lax.Precision.HIGH
FULL = lax.Precision.HIGHEST


def nn(a, b, precision=FULL):
    return lax.dot_general(
        a, b, (((1,), (0,)), ((), ())), precision=precision, preferred_element_type=F32
    )


def nt(a, b, precision=FULL):
    return lax.dot_general(
        a, b, (((1,), (1,)), ((), ())), precision=precision, preferred_element_type=F32
    )


def two_parts(x):
    top = x.astype(BF16)
    return top, (x - top.astype(F32)).astype(BF16)


def one_hot_rows(count, index):
    return lax.broadcasted_iota(jnp.int32, (count, LANES), 0) == index


def from_behind(array, axis, by):
    length = lax.axis_size(axis)
    pairs = [(i, i + by) for i in range(length) if 0 <= i + by < length]
    return lax.ppermute(array, axis, pairs)


def prep_kernel(
    fronts, slot, front_ref, ranks_ref, signs_hbm, sources_hbm, dinv_hbm, ut_hbm, vt_hbm, dobs_hbm, map_hbm,
    wave_ref, adj_ref, ld_ref, e_ref, rd_ref, s_ref, t_ref, back_ref, place_ref, offset_ref,
    signs_v, sources_v, dinv_v, ut_v, vt_v, dobs_v, map_v, small_sem, block_sem,
):
    blocks, rank_max, width = ut_v.shape
    shots = signs_v.shape[0]
    groups = map_v.shape[0]
    start = pl.multiple_of(front_ref[0] * groups, groups)
    small = [
        pltpu.make_async_copy(map_hbm.at[pl.ds(start, groups)], map_v, small_sem.at[0]),
        pltpu.make_async_copy(signs_hbm, signs_v, small_sem.at[1]),
        pltpu.make_async_copy(ut_hbm, ut_v, small_sem.at[2]),
        pltpu.make_async_copy(vt_hbm, vt_v, small_sem.at[3]),
        pltpu.make_async_copy(dobs_hbm, dobs_v, small_sem.at[4]),
    ]
    for copy in small:
        copy.start()
    large = []
    for k in range(blocks):
        columns = pl.ds(k * width, width)
        pair = [
            pltpu.make_async_copy(sources_hbm.at[:, columns], sources_v.at[:, columns], block_sem.at[0, k]),
            pltpu.make_async_copy(dinv_hbm.at[k], dinv_v.at[k], block_sem.at[1, k]),
        ]
        for copy in pair:
            copy.start()
        large.append(pair)

    small[0].wait()
    cells = map_v[...]
    owner = cells >> (MC_DEV.bit_length() - 1)
    local = cells & (MC_DEV - 1)
    member = jnp.concatenate(
        [one_hot_rows(fronts, owner[j : j + 1]).astype(F32) for j in range(groups)], axis=0
    )
    member_b = member.astype(BF16)
    count = fronts * groups
    row = lax.broadcasted_iota(jnp.int32, (LANES, LANES), 0)
    lane = lax.broadcasted_iota(jnp.int32, (LANES, LANES), 1)
    before = (row < lane).astype(F32).astype(BF16)
    inside = nn(member_b, before, None)
    total = nn(member_b, jnp.ones((LANES, LANES), BF16), None)
    p = lax.broadcasted_iota(jnp.int32, (count, count), 0)
    q = lax.broadcasted_iota(jnp.int32, (count, count), 1)
    same = ((p & (fronts - 1)) == (q & (fronts - 1))) & (q < p)
    earlier = nn(same.astype(F32).astype(BF16), total.astype(BF16), None)
    ranked = member * (inside + earlier)
    place = jnp.concatenate(
        [jnp.sum(ranked[j * fronts : (j + 1) * fronts], axis=0, keepdims=True) for j in range(groups)], axis=0
    ).astype(jnp.int32) + owner * slot
    place_ref[...] = place
    high, low = place >> 7, place & (LANES - 1)
    out_rows = fronts * slot // LANES
    coarse = (local >> 7).astype(F32)
    fine = (local & (LANES - 1)).astype(F32)
    table, pick = [], []
    for j in range(groups):
        hit = one_hot_rows(out_rows, high[j : j + 1])
        table.append(
            jnp.concatenate(
                [jnp.where(hit, coarse[j : j + 1], 0.0), jnp.where(hit, fine[j : j + 1], 0.0)], axis=0
            ).astype(BF16)
        )
        pick.append(one_hot_rows(LANES, low[j : j + 1]).astype(F32).astype(BF16))
    found = nt(jnp.concatenate(table, axis=1), jnp.concatenate(pick, axis=1), None)
    offset_ref[...] = found[:out_rows] * float(LANES) + found[out_rows:]

    for copy in small[1:]:
        copy.wait()
    sign = signs_v[...].astype(F32).astype(BF16)
    rank_row = lax.broadcasted_iota(jnp.int32, (rank_max, width), 0)
    unit_row = lax.broadcasted_iota(jnp.int32, (rank_max, rank_max), 0)
    unit_lane = lax.broadcasted_iota(jnp.int32, (rank_max, rank_max), 1)
    unit = (unit_row == unit_lane).astype(F32)
    zero = jnp.zeros((shots, rank_max), F32)
    state = jnp.concatenate([zero, unit], axis=0)
    maps, pushes = [], []
    for k in range(blocks):
        for copy in large[k]:
            copy.wait()
        columns = slice(k * width, (k + 1) * width)
        source = nn(sign, sources_v[:, columns], None)
        inverse = dinv_v[k]
        left = jnp.where(rank_row < ranks_ref[k], ut_v[k], 0.0)
        swept = nt(jnp.concatenate([source, left], axis=0), inverse)
        wave, ld = swept[:shots], swept[shots:]
        wave_ref[:, columns] = wave
        ld_ref[k] = ld
        residual = wave - dobs_v[:, columns].astype(F32)
        both = jnp.concatenate([residual, ld], axis=0)
        if k + 1 < blocks:
            right = jnp.where(rank_row < ranks_ref[k + 1], vt_v[k + 1], 0.0)
            returned = nn(jnp.concatenate([both, right], axis=0), inverse, HIGH)
            rd_ref[k] = returned[shots + rank_max :]
        else:
            returned = nn(both, inverse, HIGH)
        adj_ref[:, columns] = returned[:shots]
        e_ref[k] = returned[shots : shots + rank_max]
        seen = nt(both, ld)
        s_ref[k] = state
        turned = nn(state, seen[shots:])
        pushes.append(jnp.concatenate([seen[:shots], jnp.zeros_like(unit)], axis=0) - turned)
        if k + 1 < blocks:
            passed = nt(swept, right)
            forward = -passed[shots:]
            maps.append(forward)
            state = nn(state, forward) + jnp.concatenate([passed[:shots], jnp.zeros_like(unit)], axis=0)

    back = jnp.concatenate([pushes[-1], unit], axis=0)
    for k in range(blocks - 2, -1, -1):
        t_ref[k] = back
        back = nt(back, maps[k]) + jnp.concatenate([pushes[k], jnp.zeros_like(unit)], axis=0)
    back_ref[...] = back[: shots + rank_max]


def send_kernel(fronts, slot, wave_ref, ld_ref, s_ref, next_ref, back_ref, offset_ref, send_ref, last_ref):
    rank_max, width = next_ref.shape
    shots = wave_ref.shape[0]
    blocks = ld_ref.shape[0]
    right = next_ref[...]
    swept = jnp.concatenate([wave_ref[:, (blocks - 1) * width :], ld_ref[blocks - 1]], axis=0)
    passed = nt(swept, right)
    forward = -passed[shots:]
    last_ref[...] = forward
    state = nn(s_ref[blocks - 1], forward)
    back = back_ref[...]
    payload = jnp.concatenate(
        [state[shots:], state[:shots] + passed[:shots], back[shots:], back[:shots]], axis=1
    )
    each = slot // LANES
    for g in range(fronts):
        send_ref[g, :rank_max] = payload
        send_ref[g, rank_max : rank_max + each] = offset_ref[g * each : (g + 1) * each]


def solve_kernel(
    fronts, slot, ranks_of_rhs, front_ref, got_ref, wave_ref, adj_ref, ld_ref, e_ref, rd_ref, s_ref, t_ref,
    next_ref, last_ref, place_ref, dinv_hbm,
    wave_out, adj_out, image_out,
    ahead_v, behind_v, dinv_v, image_v, sem,
):
    blocks, rank_max, width = ld_ref.shape
    shots = wave_ref.shape[0]
    fetch = pltpu.make_async_copy(dinv_hbm.at[blocks - 1], dinv_v, sem)
    fetch.start()
    mine = front_ref[0]
    n = rank_max

    def step_forward(g, state):
        ahead_v[g] = state
        return nn(state, got_ref[g, :n, :n]) + got_ref[g, :n, n : 2 * n]

    def step_backward(i, state):
        g = fronts - 1 - i
        behind_v[g] = state
        push = got_ref[g, :n, 3 * n : 4 * n] + nn(ahead_v[g], got_ref[g, :n, 2 * n : 3 * n])
        return nt(state, got_ref[g, :n, :n]) + push

    zero = jnp.zeros((shots, rank_max), F32)
    lax.fori_loop(0, fronts, step_forward, zero, unroll=True)
    lax.fori_loop(0, fronts, step_backward, zero, unroll=True)
    ahead = ahead_v[mine]
    behind = behind_v[mine]
    turned = nt(behind, last_ref[...])
    fetch.wait()
    rd_last = nn(next_ref[...], dinv_v[...], HIGH)
    scale = 1.0 / (shots * ranks_of_rhs)
    for k in range(blocks):
        columns = slice(k * width, (k + 1) * width)
        s = s_ref[k, :shots] + nn(ahead, s_ref[k, shots:])
        wave = wave_ref[:, columns] - nn(s, ld_ref[k], HIGH)
        if k + 1 < blocks:
            t = t_ref[k]
            arriving = t[:shots] + nn(ahead, t[shots : shots + n]) + nn(turned, t[shots + n :])
            rd = rd_ref[k]
        else:
            arriving = behind
            rd = rd_last
        adj = adj_ref[:, columns] - nn(s, e_ref[k], HIGH) - nn(arriving, rd, HIGH)
        wave_out[:, columns] = wave
        adj_out[:, columns] = adj
        image_v[:, columns] = jnp.sum(wave * adj, axis=0, keepdims=True) * scale

    groups = place_ref.shape[0]
    place = place_ref[...]
    high, low = place >> 7, place & (LANES - 1)
    out_rows = fronts * slot // LANES
    tops, rests, pick = [], [], []
    for j in range(groups):
        hit = one_hot_rows(out_rows, high[j : j + 1])
        top, rest = two_parts(jnp.where(hit, image_v[:, j * LANES : (j + 1) * LANES], 0.0))
        tops.append(top)
        rests.append(rest)
        pick.append(one_hot_rows(LANES, low[j : j + 1]).astype(F32).astype(BF16))
    table = jnp.concatenate([jnp.concatenate(tops, axis=1), jnp.concatenate(rests, axis=1)], axis=0)
    packed = nt(table, jnp.concatenate(pick, axis=1), None)
    packed = packed[:out_rows] + packed[out_rows:]
    each = slot // LANES
    for g in range(fronts):
        for r in range(ranks_of_rhs):
            image_out[g * ranks_of_rhs + r] = packed[g * each : (g + 1) * each]


def gather_kernel(fronts, slot, ranks_of_rhs, rank_max, got_ref, terms_ref, out_ref):
    each = slot // LANES
    out_rows = MC_DEV // LANES
    tops, rests, pick = [], [], []
    for g in range(fronts):
        terms = terms_ref[g * ranks_of_rhs]
        for r in range(1, ranks_of_rhs):
            terms = terms + terms_ref[g * ranks_of_rhs + r]
        cells = got_ref[g, rank_max : rank_max + each].astype(jnp.int32)
        high, low = cells >> 7, cells & (LANES - 1)
        for j in range(each):
            hit = one_hot_rows(out_rows, high[j : j + 1])
            top, rest = two_parts(jnp.where(hit, terms[j : j + 1], 0.0))
            tops.append(top)
            rests.append(rest)
            pick.append(one_hot_rows(LANES, low[j : j + 1]).astype(F32).astype(BF16))
    table = jnp.concatenate([jnp.concatenate(tops, axis=1), jnp.concatenate(rests, axis=1)], axis=0)
    found = nt(table, jnp.concatenate(pick, axis=1), None)
    out_ref[...] = found[:out_rows] + found[out_rows:]


def body(signs, sources, dinv, u_fac, v_fac, ranks, dobs, cellmap):
    shots = signs.shape[0]
    blocks, width, rank_max = u_fac.shape
    rows = blocks * width
    fronts = lax.axis_size("front")
    rhs = lax.axis_size("rhs")
    cap = 2 * rows // fronts
    slot = (cap + LANES - 1) // LANES * LANES
    each = slot // LANES
    packed_rows = fronts * each
    groups = rows // LANES
    tall = (rank_max + each + 7) // 8 * 8
    front = lax.axis_index("front").astype(jnp.int32).reshape(1)
    ut = jnp.swapaxes(u_fac, 1, 2)
    vt = jnp.swapaxes(v_fac, 1, 2)
    first = jnp.where(jnp.arange(rank_max)[:, None] < ranks[0], vt[0], 0.0)
    following = from_behind(first, "front", -1)

    smem = pl.BlockSpec(memory_space=pltpu.SMEM)
    vmem = pl.BlockSpec(memory_space=pltpu.VMEM)
    hbm = pl.BlockSpec(memory_space=pl.ANY)

    def shape(*dims):
        return jax.ShapeDtypeStruct(dims, F32)

    wave, adj, ld, e, rd, s, t, back, place, offset = pl.pallas_call(
        functools.partial(prep_kernel, fronts, slot),
        name="prep",
        out_shape=(
            shape(shots, rows),
            shape(shots, rows),
            shape(blocks, rank_max, width),
            shape(blocks, rank_max, width),
            shape(blocks - 1, rank_max, width),
            shape(blocks, shots + rank_max, rank_max),
            shape(blocks - 1, shots + 2 * rank_max, rank_max),
            shape(shots + rank_max, rank_max),
            jax.ShapeDtypeStruct((groups, LANES), jnp.int32),
            shape(packed_rows, LANES),
        ),
        in_specs=[smem, smem] + [hbm] * 7,
        out_specs=[vmem] * 10,
        scratch_shapes=[
            pltpu.VMEM(signs.shape, signs.dtype),
            pltpu.VMEM(sources.shape, sources.dtype),
            pltpu.VMEM(dinv.shape, dinv.dtype),
            pltpu.VMEM(ut.shape, ut.dtype),
            pltpu.VMEM(vt.shape, vt.dtype),
            pltpu.VMEM(dobs.shape, dobs.dtype),
            pltpu.VMEM((groups, LANES), cellmap.dtype),
            pltpu.SemaphoreType.DMA((5,)),
            pltpu.SemaphoreType.DMA((2, blocks)),
        ],
        cost_estimate=pl.CostEstimate(flops=400_000_000, bytes_accessed=6_000_000, transcendentals=0),
    )(front, ranks, signs, sources, dinv, ut, vt, dobs, cellmap.reshape(-1, LANES))

    send, last = pl.pallas_call(
        functools.partial(send_kernel, fronts, slot),
        name="send",
        out_shape=(shape(fronts, tall, LANES), shape(rank_max, rank_max)),
        in_specs=[vmem] * 6,
        out_specs=[vmem] * 2,
    )(wave, ld, s, following, back, offset)

    got = lax.all_to_all(send, "front", 0, 0)

    wave, adj, image = pl.pallas_call(
        functools.partial(solve_kernel, fronts, slot, rhs),
        name="solve",
        out_shape=(shape(shots, rows), shape(shots, rows), shape(fronts * rhs, each, LANES)),
        in_specs=[smem] + [vmem] * 11 + [hbm],
        out_specs=[vmem] * 3,
        scratch_shapes=[
            pltpu.VMEM((fronts, shots, rank_max), F32),
            pltpu.VMEM((fronts, shots, rank_max), F32),
            pltpu.VMEM((width, width), F32),
            pltpu.VMEM((1, rows), F32),
            pltpu.SemaphoreType.DMA,
        ],
    )(front, got, wave, adj, ld, e, rd, s, t, following, last, place, dinv)

    terms = lax.all_to_all(image, ("front", "rhs"), 0, 0)

    gradient = pl.pallas_call(
        functools.partial(gather_kernel, fronts, slot, rhs, rank_max),
        name="gather",
        out_shape=shape(MC_DEV // LANES, LANES),
        in_specs=[vmem] * 2,
        out_specs=vmem,
    )(got, terms)
    return (wave, adj, gradient.reshape(MC_DEV))


def solution(mesh):
    in_specs = (
        P("rhs", None),
        P(None, "front"),
        P("front", None, None),
        P("front", None, None),
        P("front", None, None),
        P("front"),
        P("rhs", "front"),
        P(),
    )
    out_specs = (P("rhs", "front"), P("rhs", "front"), P("front"))
    return jax.shard_map(body, mesh=mesh, in_specs=in_specs, out_specs=out_specs, check_vma=False)
```

```python
import functools

import jax
import jax.numpy as jnp
from jax import lax
from jax.experimental import pallas as pl
from jax.experimental.pallas import tpu as pltpu
from jax.sharding import PartitionSpec as P

MC_DEV = 8192
LANES = 128
F32 = jnp.float32
BF16 = jnp.bfloat16
NN = (((1,), (0,)), ((), ()))
NT = (((1,), (1,)), ((), ()))


def dot(a, b, dims=NN):
    return lax.dot_general(a, b, dims, preferred_element_type=F32)


def parts(x):
    top = x.astype(BF16)
    return top, (x - top.astype(F32)).astype(BF16)


def dot3(a, b, dims=NN):
    rows = a[0].shape[0]
    first = dot(jnp.concatenate(a, axis=0), b[0], dims)
    return first[:rows] + first[rows:] + dot(a[0], b[1], dims)


def rows_of(pair, start, stop):
    return pair[0][start:stop], pair[1][start:stop]


def hits(count, index):
    return lax.broadcasted_iota(jnp.int32, (count, LANES), 0) == index


def as_ones(mask):
    return mask.astype(F32).astype(BF16)


def from_behind(array, axis, by):
    length = lax.axis_size(axis)
    pairs = [(i, i + by) for i in range(length) if 0 <= i + by < length]
    return lax.ppermute(array, axis, pairs)


def prep_kernel(
    ranks_hbm, signs_hbm, sources_hbm, dinv_hbm, ut_hbm, vt_hbm, dobs_hbm,
    y_ref, maps_ref, back_ref,
    ranks_ref, signs_v, sources_v, dinv_v, ut_v, vt_v, dobs_v, small_sem, block_sem,
):
    blocks, rank_max, width = ut_v.shape
    shots = signs_v.shape[0]
    small = [
        pltpu.make_async_copy(signs_hbm, signs_v, small_sem.at[0]),
        pltpu.make_async_copy(ut_hbm, ut_v, small_sem.at[1]),
        pltpu.make_async_copy(vt_hbm, vt_v, small_sem.at[2]),
        pltpu.make_async_copy(dobs_hbm, dobs_v, small_sem.at[3]),
        pltpu.make_async_copy(ranks_hbm, ranks_ref, small_sem.at[4]),
    ]
    large = []
    for k in range(blocks):
        columns = pl.ds(k * width, width)
        large.append(
            [
                pltpu.make_async_copy(sources_hbm.at[:, columns], sources_v.at[:, columns], block_sem.at[0, k]),
                pltpu.make_async_copy(dinv_hbm.at[k], dinv_v.at[k], block_sem.at[1, k]),
            ]
        )
    for copy in small + [copy for pair in large for copy in pair]:
        copy.start()
    for copy in small:
        copy.wait()

    sign = signs_v[...].astype(F32).astype(BF16)
    rank_row = lax.broadcasted_iota(jnp.int32, (rank_max, width), 0)
    unit_row = lax.broadcasted_iota(jnp.int32, (rank_max, rank_max), 0)
    unit_lane = lax.broadcasted_iota(jnp.int32, (rank_max, rank_max), 1)
    unit = (unit_row == unit_lane).astype(F32)
    nothing = jnp.zeros((rank_max, rank_max), F32)
    state = jnp.concatenate([jnp.zeros((shots, rank_max), F32), unit], axis=0)
    back = None
    for k in range(blocks):
        columns = slice(k * width, (k + 1) * width)
        for copy in large[k]:
            copy.wait()
        source = dot(sign, sources_v[:, columns])
        inverse = parts(dinv_v[k])
        left = jnp.where(rank_row < ranks_ref[k], ut_v[k], 0.0)
        swept = dot3(parts(jnp.concatenate([source, left], axis=0)), inverse, NT)
        y_ref[k] = swept
        residual = swept[:shots] - dobs_v[:, columns].astype(F32)
        swept = parts(swept)
        ld = rows_of(swept, shots, None)
        residual = parts(residual)
        both = tuple(jnp.concatenate([r, l], axis=0) for r, l in zip(residual, ld))
        seen = dot3(both, ld, NT)
        maps_ref[k, :, :rank_max] = state
        pair = parts(state)
        push = jnp.concatenate([seen[:shots], nothing], axis=0) - dot3(pair, parts(seen[shots:]))
        maps_ref[k, :, rank_max : 2 * rank_max] = push
        if k == 0:
            back = push
        else:
            back = back + dot3(parts(push), rows_of(pair, shots, None), NT)
        if k + 1 < blocks:
            right = jnp.where(rank_row < ranks_ref[k + 1], vt_v[k + 1], 0.0)
            passed = dot3(swept, parts(right), NT)
            forward = -passed[shots:]
            maps_ref[k, :rank_max, 2 * rank_max : 3 * rank_max] = forward
            state = dot3(pair, parts(forward)) + jnp.concatenate([passed[:shots], nothing], axis=0)
    back_ref[...] = back


def send_kernel(fronts, y_ref, maps_ref, next_ref, back_ref, send_ref, last_ref):
    blocks = y_ref.shape[0]
    shots = y_ref.shape[1] - next_ref.shape[0]
    passed = dot3(parts(y_ref[blocks - 1]), parts(next_ref[...]), NT)
    forward = -passed[shots:]
    last_ref[...] = forward
    state = dot3(parts(maps_ref[blocks - 1, :, : forward.shape[0]]), parts(forward))
    back = back_ref[...]
    payload = jnp.concatenate(
        [state[shots:], state[:shots] + passed[:shots], back[shots:], back[:shots]], axis=1
    )
    for g in range(fronts):
        send_ref[g] = payload


def fields_kernel(
    fronts, slot, front_ref, y_ref, maps_ref, next_ref, last_ref, map_hbm, dinv_hbm, vt_hbm, dobs_hbm, ranks_hbm,
    wave_ref, wave_top, wave_rest, adj_ref, ahead_top, ahead_rest, behind_top, behind_rest, hit_ref, pick_ref,
    map_v, dinv_v, vt_v, dobs_v, ranks_ref, sem, block_sem,
):
    blocks, n, width = vt_v.shape
    shots = dobs_v.shape[0]
    groups = map_v.shape[0]
    start = pl.multiple_of(front_ref[0] * groups, groups)
    fetch = [
        pltpu.make_async_copy(vt_hbm, vt_v, sem.at[0]),
        pltpu.make_async_copy(dobs_hbm, dobs_v, sem.at[1]),
        pltpu.make_async_copy(ranks_hbm, ranks_ref, sem.at[2]),
        pltpu.make_async_copy(map_hbm.at[pl.ds(start, groups)], map_v, sem.at[3]),
    ]
    for copy in fetch:
        copy.start()
    large = [pltpu.make_async_copy(dinv_hbm.at[k], dinv_v.at[k], block_sem.at[k]) for k in range(blocks)]
    for copy in large:
        copy.start()

    unit_row = lax.broadcasted_iota(jnp.int32, (n, n), 0)
    unit_lane = lax.broadcasted_iota(jnp.int32, (n, n), 1)
    unit = (unit_row == unit_lane).astype(F32)
    nothing = jnp.zeros((n, n), F32)
    state = jnp.concatenate([jnp.zeros((shots + n, n), F32), unit], axis=0)
    backs = [None] * blocks
    for k in range(blocks - 1, 0, -1):
        backs[k] = state
        factor = parts(last_ref[...] if k + 1 == blocks else maps_ref[k, :n, 2 * n : 3 * n])
        state = dot3(parts(state), factor, NT) + jnp.concatenate([maps_ref[k, :, n : 2 * n], nothing], axis=0)
    backs[0] = state
    for copy in fetch:
        copy.wait()
    rank_row = lax.broadcasted_iota(jnp.int32, (n, width), 0)

    for k in range(blocks):
        columns = slice(k * width, (k + 1) * width)
        if k + 1 < blocks:
            right = jnp.where(rank_row < ranks_ref[k + 1], vt_v[k + 1], 0.0)
        else:
            right = next_ref[...]
        residual = y_ref[k, :shots] - dobs_v[:, columns].astype(F32)
        rows = jnp.concatenate([residual, y_ref[k, shots:], right], axis=0)
        large[k].wait()
        returned = dot3(parts(rows), parts(dinv_v[k]))
        ahead = parts(maps_ref[k, :, :n])
        wave = dot3(ahead, parts(y_ref[k, shots:]))
        wave_ref[:, columns] = y_ref[k, :shots] - wave[:shots]
        wave_top[:, columns], wave_rest[:, columns] = parts(-wave[shots:])
        adj = dot3(ahead, parts(returned[shots : shots + n]))
        factor = parts(backs[k] if k else backs[0])
        late = dot3(factor, parts(returned[shots + n :]))
        adj_ref[:, columns] = returned[:shots] - adj[:shots] - late[:shots]
        ahead_top[:, columns], ahead_rest[:, columns] = parts(-adj[shots:] - late[shots : shots + n])
        behind_top[:, columns], behind_rest[:, columns] = parts(-late[shots + n :])

    owner = map_v[...] >> (MC_DEV.bit_length() - 1)
    member = jnp.concatenate([hits(fronts, owner[j : j + 1]).astype(F32) for j in range(groups)], axis=0)
    ranked = member * rank_in_order(member, fronts, groups, False)
    place = jnp.concatenate(
        [jnp.sum(ranked[j * fronts : (j + 1) * fronts], axis=0, keepdims=True) for j in range(groups)], axis=0
    ).astype(jnp.int32) + owner * slot
    out_rows = hit_ref.shape[0]
    for j in range(groups):
        lanes = slice(j * LANES, (j + 1) * LANES)
        at = place[j : j + 1]
        hit_ref[:, lanes] = as_ones(hits(out_rows, at >> 7))
        pick_ref[:, lanes] = as_ones(hits(LANES, at & (LANES - 1)))


def rank_in_order(member, stride, groups, blocked):
    count = member.shape[0]
    row = lax.broadcasted_iota(jnp.int32, (LANES, LANES), 0)
    lane = lax.broadcasted_iota(jnp.int32, (LANES, LANES), 1)
    member = member.astype(BF16)
    inside = dot(member, as_ones(row < lane))
    total = dot(member, jnp.ones((LANES, LANES), BF16))
    p = lax.broadcasted_iota(jnp.int32, (count, count), 0)
    q = lax.broadcasted_iota(jnp.int32, (count, count), 1)
    if blocked:
        shift = groups.bit_length() - 1
        same = (p >> shift) == (q >> shift)
    else:
        same = (p & (stride - 1)) == (q & (stride - 1))
    return inside + dot(as_ones(same & (q < p)), total.astype(BF16))


def solve_kernel(
    fronts, rhs, front_ref, got_ref, wave_ref, wave_top, wave_rest, adj_ref, ahead_top, ahead_rest,
    behind_top, behind_rest, hit_ref, pick_ref,
    wave_out, adj_out, image_out, token_ref,
    ahead_v, behind_v,
):
    shots, rows = wave_ref.shape
    n = wave_top.shape[0]
    mine = front_ref[0]
    token_ref[...] = jnp.zeros_like(token_ref)
    zero = jnp.zeros((shots, n), F32)

    state = zero
    ahead_v[0] = state
    pushes = [None]
    maps = [None]
    for g in range(fronts):
        if g > 0:
            ahead_v[g] = state
            pushes.append(dot3(parts(state), parts(got_ref[g, :, 2 * n : 3 * n])) + got_ref[g, :, 3 * n :])
            maps.append(parts(got_ref[g, :, :n]))
        if g + 1 < fronts:
            here = got_ref[g, :, n : 2 * n]
            state = here if g == 0 else dot3(parts(state), maps[g]) + here
    state = zero
    for g in range(fronts - 1, -1, -1):
        behind_v[g] = state
        if g > 0:
            here = pushes[g]
            state = here if g + 1 == fronts else dot3(parts(state), maps[g], NT) + here

    ahead = parts(ahead_v[mine])
    wave = wave_ref[...] + dot3(ahead, (wave_top[...], wave_rest[...]))
    wave_out[...] = wave
    adj = adj_ref[...] + dot3(ahead, (ahead_top[...], ahead_rest[...]))
    adj = adj + dot3(parts(behind_v[mine]), (behind_top[...], behind_rest[...]))
    adj_out[...] = adj
    image = jnp.sum(wave * adj, axis=0, keepdims=True) * (1.0 / (shots * rhs))
    top, rest = parts(image)
    hit = hit_ref[...]
    out_rows = hit.shape[0]
    table = jnp.concatenate([hit * top, hit * rest], axis=0)
    packed = dot(table, pick_ref[...], NT)
    packed = packed[:out_rows] + packed[out_rows:]
    each = out_rows // fronts
    for g in range(fronts):
        for r in range(rhs):
            image_out[g * rhs + r] = packed[g * each : (g + 1) * each]


def table_kernel(fronts, slot, front_ref, map_ref, token_ref, hit_ref, pick_ref):
    del token_ref
    each = slot // LANES
    count = map_ref.shape[0]
    groups = count // fronts
    cells = map_ref[...]
    mine = (cells >> (MC_DEV.bit_length() - 1)) == front_ref[0]
    rank = rank_in_order(mine.astype(F32), fronts, groups, True).astype(jnp.int32)
    rank = jnp.where(mine, rank, -1)
    local = cells & (MC_DEV - 1)
    coarse = (local >> 7).astype(F32)
    fine = (local & (LANES - 1)).astype(F32)
    high = rank >> 7
    low = jnp.where(mine, rank & (LANES - 1), -1)
    for f in range(fronts):
        table, pick = [], []
        for j in range(f * groups, (f + 1) * groups):
            hit = hits(each, high[j : j + 1])
            table.append(
                jnp.concatenate(
                    [jnp.where(hit, coarse[j : j + 1], 0.0), jnp.where(hit, fine[j : j + 1], 0.0)], axis=0
                ).astype(BF16)
            )
            pick.append(as_ones(hits(LANES, low[j : j + 1])))
        found = dot(jnp.concatenate(table, axis=1), jnp.concatenate(pick, axis=1), NT).astype(jnp.int32)
        for j in range(each):
            lanes = slice((f * each + j) * LANES, (f * each + j + 1) * LANES)
            hit_ref[:, lanes] = as_ones(hits(MC_DEV // LANES, found[j : j + 1]))
            pick_ref[:, lanes] = as_ones(hits(LANES, found[each + j : each + j + 1]))


def gather_kernel(fronts, rhs, terms_ref, hit_ref, pick_ref, out_ref):
    each = terms_ref.shape[1]
    rows = []
    for g in range(fronts):
        terms = terms_ref[g * rhs]
        for r in range(1, rhs):
            terms = terms + terms_ref[g * rhs + r]
        rows += [terms[j : j + 1] for j in range(each)]
    top, rest = parts(jnp.concatenate(rows, axis=1))
    hit = hit_ref[...]
    out_rows = hit.shape[0]
    found = dot(jnp.concatenate([hit * top, hit * rest], axis=0), pick_ref[...], NT)
    out_ref[...] = found[:out_rows] + found[out_rows:]


def body(signs, sources, dinv, u_fac, v_fac, ranks, dobs, cellmap):
    shots = signs.shape[0]
    blocks, width, n = u_fac.shape
    rows = blocks * width
    fronts = lax.axis_size("front")
    rhs = lax.axis_size("rhs")
    cap = 2 * rows // fronts
    slot = (cap + LANES - 1) // LANES * LANES
    each = slot // LANES
    groups = rows // LANES
    front = lax.axis_index("front").astype(jnp.int32).reshape(1)
    ut = jnp.swapaxes(u_fac, 1, 2)
    vt = jnp.swapaxes(v_fac, 1, 2)
    cells = cellmap.reshape(-1, LANES)
    live = jnp.clip(ranks[0] - jnp.arange(n, dtype=jnp.int32), 0, 1).astype(F32)
    following = from_behind(vt[0] * live[:, None], "front", -1)

    smem = pl.BlockSpec(memory_space=pltpu.SMEM)
    vmem = pl.BlockSpec(memory_space=pltpu.VMEM)
    hbm = pl.BlockSpec(memory_space=pltpu.HBM)

    def held(*arrays):
        return [pltpu.with_memory_space_constraint(a, pltpu.VMEM) for a in arrays]

    def far(*arrays):
        return [pltpu.with_memory_space_constraint(a, pltpu.HBM) for a in arrays]

    def cost(us):
        return pl.CostEstimate(flops=int(us * 1e9), bytes_accessed=int(us * 3e6), transcendentals=0)

    room = pltpu.CompilerParams(vmem_limit_bytes=24 * 2**20)

    y, maps, back = pl.pallas_call(
        prep_kernel,
        name="prep",
        out_shape=(
            pltpu.VMEM((blocks, shots + n, width), F32),
            pltpu.VMEM((blocks, shots + n, 4 * n), F32),
            pltpu.VMEM((shots + n, n), F32),
        ),
        in_specs=[hbm] * 7,
        out_specs=[vmem] * 3,
        scratch_shapes=[
            pltpu.SMEM(ranks.shape, ranks.dtype),
            pltpu.VMEM(signs.shape, signs.dtype),
            pltpu.VMEM(sources.shape, sources.dtype),
            pltpu.VMEM(dinv.shape, dinv.dtype),
            pltpu.VMEM(ut.shape, ut.dtype),
            pltpu.VMEM(vt.shape, vt.dtype),
            pltpu.VMEM(dobs.shape, dobs.dtype),
            pltpu.SemaphoreType.DMA((5,)),
            pltpu.SemaphoreType.DMA((2, blocks)),
        ],
        cost_estimate=cost(6),
        compiler_params=room,
    )(*far(ranks, signs, sources, dinv, ut, vt, dobs))

    send, last = pl.pallas_call(
        functools.partial(send_kernel, fronts),
        name="send",
        out_shape=(pltpu.VMEM((fronts, n, 4 * n), F32), pltpu.VMEM((n, n), F32)),
        in_specs=[vmem] * 4,
        out_specs=[vmem] * 2,
        cost_estimate=cost(0.5),
        compiler_params=room,
    )(*held(y, maps, following, back))

    got = lax.all_to_all(send, "front", 0, 0)

    fields = pl.pallas_call(
        functools.partial(fields_kernel, fronts, slot),
        name="fields",
        out_shape=(
            pltpu.VMEM((shots, rows), F32),
            pltpu.VMEM((n, rows), BF16),
            pltpu.VMEM((n, rows), BF16),
            pltpu.VMEM((shots, rows), F32),
            pltpu.VMEM((n, rows), BF16),
            pltpu.VMEM((n, rows), BF16),
            pltpu.VMEM((n, rows), BF16),
            pltpu.VMEM((n, rows), BF16),
            pltpu.VMEM((fronts * each, rows), BF16),
            pltpu.VMEM((LANES, rows), BF16),
        ),
        in_specs=[smem] + [vmem] * 4 + [hbm] * 5,
        out_specs=[vmem] * 10,
        scratch_shapes=[
            pltpu.VMEM((groups, LANES), cells.dtype),
            pltpu.VMEM(dinv.shape, dinv.dtype),
            pltpu.VMEM(vt.shape, vt.dtype),
            pltpu.VMEM(dobs.shape, dobs.dtype),
            pltpu.SMEM(ranks.shape, ranks.dtype),
            pltpu.SemaphoreType.DMA((4,)),
            pltpu.SemaphoreType.DMA((blocks,)),
        ],
        cost_estimate=cost(5),
        compiler_params=room,
    )(front, *held(y, maps, following, last), *far(cells, dinv, vt, dobs, ranks))

    wave, adj, image, token = pl.pallas_call(
        functools.partial(solve_kernel, fronts, rhs),
        name="solve",
        out_shape=(
            pltpu.VMEM((shots, rows), F32),
            pltpu.VMEM((shots, rows), F32),
            pltpu.VMEM((fronts * rhs, each, LANES), F32),
            pltpu.VMEM((8, LANES), F32),
        ),
        in_specs=[smem] + [vmem] * 11,
        out_specs=[vmem] * 4,
        scratch_shapes=[
            pltpu.VMEM((fronts, shots, n), F32),
            pltpu.VMEM((fronts, shots, n), F32),
        ],
        cost_estimate=cost(3),
        compiler_params=room,
    )(front, *held(got, *fields))

    terms = lax.all_to_all(image, ("front", "rhs"), 0, 0)

    hit, pick = pl.pallas_call(
        functools.partial(table_kernel, fronts, slot),
        name="tables",
        out_shape=(
            pltpu.VMEM((MC_DEV // LANES, fronts * slot), BF16),
            pltpu.VMEM((LANES, fronts * slot), BF16),
        ),
        in_specs=[smem, vmem, vmem],
        out_specs=[vmem] * 2,
        cost_estimate=cost(4),
        compiler_params=room,
    )(front, *far(cells), *held(token))

    gradient = pl.pallas_call(
        functools.partial(gather_kernel, fronts, rhs),
        name="gather",
        out_shape=jax.ShapeDtypeStruct((MC_DEV // LANES, LANES), F32),
        in_specs=[vmem] * 3,
        out_specs=vmem,
        cost_estimate=cost(1),
        compiler_params=room,
    )(*held(terms, hit, pick))
    return (wave, adj, gradient.reshape(MC_DEV))


def solution(mesh):
    in_specs = (
        P("rhs", None),
        P(None, "front"),
        P("front", None, None),
        P("front", None, None),
        P("front", None, None),
        P("front"),
        P("rhs", "front"),
        P(),
    )
    out_specs = (P("rhs", "front"), P("rhs", "front"), P("front"))
    return jax.shard_map(body, mesh=mesh, in_specs=in_specs, out_specs=out_specs, check_vma=False)
```

```python
import functools

import jax
import jax.numpy as jnp
import numpy as np
from jax import lax
from jax.experimental import pallas as pl
from jax.experimental.pallas import tpu as pltpu
from jax.sharding import PartitionSpec as P

MC_DEV = 8192
LANES = 128
F32 = jnp.float32
BF16 = jnp.bfloat16
NN = (((1,), (0,)), ((), ()))
NT = (((1,), (1,)), ((), ()))


def dot(a, b, dims=NN):
    return lax.dot_general(a, b, dims, preferred_element_type=F32)


def parts(x):
    top = x.astype(BF16)
    return top, (x - top.astype(F32)).astype(BF16)


def dot3(a, b, dims=NN):
    rows = a[0].shape[0]
    first = dot(jnp.concatenate(a, axis=0), b[0], dims)
    return first[:rows] + first[rows:] + dot(a[0], b[1], dims)


def rows_of(pair, start, stop):
    return pair[0][start:stop], pair[1][start:stop]


def hits(count, index):
    return lax.broadcasted_iota(jnp.int32, (count, LANES), 0) == index


def as_ones(mask):
    return mask.astype(F32).astype(BF16)


def from_behind(array, axis, by):
    length = lax.axis_size(axis)
    pairs = [(i, i + by) for i in range(length) if 0 <= i + by < length]
    return lax.ppermute(array, axis, pairs)


def prep_kernel(
    ranks_hbm, signs_hbm, sources_hbm, dinv_hbm, ut_hbm, vt_hbm, dobs_hbm,
    y_ref, maps_ref, back_ref,
    ranks_ref, signs_v, sources_v, dinv_v, ut_v, vt_v, dobs_v, small_sem, block_sem,
):
    blocks, rank_max, width = ut_v.shape
    shots = signs_v.shape[0]
    small = [
        pltpu.make_async_copy(signs_hbm, signs_v, small_sem.at[0]),
        pltpu.make_async_copy(ut_hbm, ut_v, small_sem.at[1]),
        pltpu.make_async_copy(vt_hbm, vt_v, small_sem.at[2]),
        pltpu.make_async_copy(dobs_hbm, dobs_v, small_sem.at[3]),
        pltpu.make_async_copy(ranks_hbm, ranks_ref, small_sem.at[4]),
    ]
    large = []
    for k in range(blocks):
        columns = pl.ds(k * width, width)
        large.append(
            [
                pltpu.make_async_copy(sources_hbm.at[:, columns], sources_v.at[:, columns], block_sem.at[0, k]),
                pltpu.make_async_copy(dinv_hbm.at[k], dinv_v.at[k], block_sem.at[1, k]),
            ]
        )
    early = small[:1] + [pair[0] for pair in large]
    late = small[1:] + [pair[1] for pair in large]
    for copy in early + late:
        copy.start()
    for copy in early:
        copy.wait()

    sign = signs_v[...].astype(F32).astype(BF16)
    rank_row = lax.broadcasted_iota(jnp.int32, (rank_max, width), 0)
    products = {}
    for k in range(blocks):
        y_ref[k, :shots] = dot(sign, sources_v[:, k * width : (k + 1) * width])
    for copy in late:
        copy.wait()

    def sweep(k):
        left = jnp.where(rank_row < ranks_ref[k], ut_v[k], 0.0)
        y_ref[k] = dot3(parts(jnp.concatenate([y_ref[k, :shots], left], axis=0)), parts(dinv_v[k]), NT)

    def project(k):
        swept = y_ref[k]
        residual = parts(swept[:shots] - dobs_v[:, k * width : (k + 1) * width].astype(F32))
        swept = parts(swept)
        wave, ld = rows_of(swept, 0, shots), rows_of(swept, shots, None)
        if k + 1 < blocks:
            right = parts(jnp.where(rank_row < ranks_ref[k + 1], vt_v[k + 1], 0.0))
        else:
            right = parts(jnp.zeros((rank_max, width), F32))
        rows = tuple(jnp.concatenate(three, axis=0) for three in zip(wave, residual, ld))
        products[k] = dot3(rows, tuple(jnp.concatenate(two, axis=0) for two in zip(right, ld)), NT)

    for k in range(blocks):
        sweep(k)
    for k in range(blocks):
        project(k)

    n = rank_max
    nothing = jnp.zeros((n, n), F32)

    def follow(span, k):
        later = dot3(span, parts(steps[k][shots:]))
        return jnp.concatenate([later[:shots] + steps[k][:shots], later[shots:]], axis=0)

    steps = [jnp.concatenate([seen[:shots, :n], -seen[2 * shots :, :n]], axis=0) for seen in map(products.get, range(blocks))]
    joint = {k: follow(parts(steps[k]), k + 1) for k in range(1, blocks - 2, 2)}
    spans = [steps[0]]
    for k in range(1, blocks - 1, 2):
        pair = parts(spans[-1])
        spans.append(follow(pair, k))
        if k in joint:
            later = dot3(pair, parts(joint[k][shots:]))
            spans.append(jnp.concatenate([later[:shots] + joint[k][:shots], later[shots:]], axis=0))
    back = None
    for k in range(blocks):
        seen = products[k]
        push = jnp.concatenate([seen[shots : 2 * shots, n:], nothing], axis=0)
        if k == 0:
            push = push - jnp.concatenate([nothing, seen[2 * shots :, n:]], axis=0)
            back = push
        else:
            pair = parts(spans[k - 1])
            push = push - dot3(pair, parts(seen[2 * shots :, n:]))
            back = back + dot3(parts(push), rows_of(pair, shots, None), NT)
        if k + 1 < blocks:
            maps_ref[k, :, :n] = spans[k]
        maps_ref[k, :, n : 2 * n] = push
        maps_ref[k, :n, 2 * n :] = seen[2 * shots :]
    back_ref[...] = back


def send_kernel(fronts, y_ref, maps_ref, next_ref, back_ref, send_ref, last_ref):
    blocks = y_ref.shape[0]
    shots = y_ref.shape[1] - next_ref.shape[0]
    passed = dot3(parts(y_ref[blocks - 1]), parts(next_ref[...]), NT)
    forward = -passed[shots:]
    last_ref[...] = forward
    state = dot3(parts(maps_ref[blocks - 2, :, : forward.shape[0]]), parts(forward))
    back = back_ref[...]
    payload = jnp.concatenate(
        [state[shots:], state[:shots] + passed[:shots], back[shots:], back[:shots]], axis=1
    )
    for g in range(fronts):
        send_ref[g] = payload


def fields_kernel(
    fronts, slot, front_ref, y_ref, maps_ref, next_ref, last_ref, map_hbm, dinv_hbm, vt_hbm, dobs_hbm, ranks_hbm,
    wave_ref, wave_top, wave_rest, adj_ref, ahead_top, ahead_rest, behind_top, behind_rest, hit_ref, pick_ref,
    map_v, dinv_v, vt_v, dobs_v, ranks_ref, sem, block_sem,
):
    blocks, n, width = vt_v.shape
    shots = dobs_v.shape[0]
    groups = map_v.shape[0]
    start = pl.multiple_of(front_ref[0] * groups, groups)
    fetch = [
        pltpu.make_async_copy(vt_hbm, vt_v, sem.at[0]),
        pltpu.make_async_copy(dobs_hbm, dobs_v, sem.at[1]),
        pltpu.make_async_copy(ranks_hbm, ranks_ref, sem.at[2]),
        pltpu.make_async_copy(map_hbm.at[pl.ds(start, groups)], map_v, sem.at[3]),
    ]
    for copy in fetch:
        copy.start()
    large = [pltpu.make_async_copy(dinv_hbm.at[k], dinv_v.at[k], block_sem.at[k]) for k in range(blocks)]
    for copy in large:
        copy.start()

    unit_row = lax.broadcasted_iota(jnp.int32, (n, n), 0)
    unit_lane = lax.broadcasted_iota(jnp.int32, (n, n), 1)
    unit = (unit_row == unit_lane).astype(F32)
    nothing = jnp.zeros((n, n), F32)
    state = jnp.concatenate([jnp.zeros((shots + n, n), F32), unit], axis=0)
    backs = [None] * blocks
    for k in range(blocks - 1, 0, -1):
        backs[k] = state
        factor = parts(last_ref[...] if k + 1 == blocks else -maps_ref[k, :n, 2 * n : 3 * n])
        state = dot3(parts(state), factor, NT) + jnp.concatenate([maps_ref[k, :, n : 2 * n], nothing], axis=0)
    backs[0] = state
    for copy in fetch:
        copy.wait()

    owner = map_v[...] >> (MC_DEV.bit_length() - 1)
    member = jnp.concatenate([hits(fronts, owner[j : j + 1]).astype(F32) for j in range(groups)], axis=0)
    ranked = member * rank_in_order(member, fronts, groups, False)
    place = jnp.concatenate(
        [jnp.sum(ranked[j * fronts : (j + 1) * fronts], axis=0, keepdims=True) for j in range(groups)], axis=0
    ).astype(jnp.int32) + owner * slot
    out_rows = hit_ref.shape[0]
    for j in range(groups):
        lanes = slice(j * LANES, (j + 1) * LANES)
        at = place[j : j + 1]
        hit_ref[:, lanes] = as_ones(hits(out_rows, at >> 7))
        pick_ref[:, lanes] = as_ones(hits(LANES, at & (LANES - 1)))

    for copy in large:
        copy.wait()
    rank_row = lax.broadcasted_iota(jnp.int32, (n, width), 0)

    for k in range(blocks):
        columns = slice(k * width, (k + 1) * width)
        if k + 1 < blocks:
            right = jnp.where(rank_row < ranks_ref[k + 1], vt_v[k + 1], 0.0)
        else:
            right = next_ref[...]
        residual = y_ref[k, :shots] - dobs_v[:, columns].astype(F32)
        rows = jnp.concatenate([residual, y_ref[k, shots:], right], axis=0)
        returned = dot3(parts(rows), parts(dinv_v[k]))
        if k > 0:
            ahead = maps_ref[k - 1, :, :n]
        else:
            ahead = jnp.concatenate([jnp.zeros((shots, n), F32), unit], axis=0)
        wave = dot3(parts(ahead), parts(y_ref[k, shots:]))
        wave_ref[:, columns] = y_ref[k, :shots] - wave[:shots]
        wave_top[:, columns], wave_rest[:, columns] = parts(-wave[shots:])
        enters = jnp.concatenate([jnp.concatenate([ahead, nothing], axis=0), backs[k]], axis=1)
        adj = dot3(parts(enters), parts(returned[shots:]))
        adj_ref[:, columns] = returned[:shots] - adj[:shots]
        ahead_top[:, columns], ahead_rest[:, columns] = parts(-adj[shots : shots + n])
        behind_top[:, columns], behind_rest[:, columns] = parts(-adj[shots + n :])


def rank_in_order(member, stride, groups, blocked):
    count = member.shape[0]
    row = lax.broadcasted_iota(jnp.int32, (LANES, LANES), 0)
    lane = lax.broadcasted_iota(jnp.int32, (LANES, LANES), 1)
    member = member.astype(BF16)
    inside = dot(member, as_ones(row < lane))
    total = dot(member, jnp.ones((LANES, LANES), BF16))
    p = lax.broadcasted_iota(jnp.int32, (count, count), 0)
    q = lax.broadcasted_iota(jnp.int32, (count, count), 1)
    if blocked:
        shift = groups.bit_length() - 1
        same = (p >> shift) == (q >> shift)
    else:
        same = (p & (stride - 1)) == (q & (stride - 1))
    return inside + dot(as_ones(same & (q < p)), total.astype(BF16))


def solve_kernel(
    fronts, rhs, front_ref, got_ref, wave_ref, wave_top, wave_rest, adj_ref, ahead_top, ahead_rest,
    behind_top, behind_rest, hit_ref, pick_ref,
    wave_out, adj_out, image_out, token_ref,
    ahead_v, behind_v,
):
    shots, rows = wave_ref.shape
    n = wave_top.shape[0]
    mine = front_ref[0]
    token_ref[...] = jnp.zeros_like(token_ref)
    zero = jnp.zeros((shots, n), F32)

    maps = [parts(got_ref[g, :, :n]) for g in range(fronts)]
    gains = [got_ref[g, :, n : 2 * n] for g in range(fronts)]
    joint = {g: parts(dot3(maps[g], maps[g + 1])) for g in range(1, fronts - 1, 2)}
    ahead_v[0] = zero
    ahead_v[1] = gains[0]
    state = gains[0]
    pushes = [None] * fronts

    def push(g, pair):
        pushes[g] = dot3(pair, parts(got_ref[g, :, 2 * n : 3 * n])) + got_ref[g, :, 3 * n :]

    for g in range(1, fronts - 1, 2):
        pair = parts(state)
        state = dot3(pair, joint[g]) + (dot3(parts(gains[g]), maps[g + 1]) + gains[g + 1])
        push(g, pair)
        between = dot3(pair, maps[g]) + gains[g]
        ahead_v[g + 1] = between
        push(g + 1, parts(between))
        ahead_v[g + 2] = state
    push(fronts - 1, parts(state))
    behind_v[fronts - 1] = zero
    state = pushes[fronts - 1]
    behind_v[fronts - 2] = state
    for g in range(fronts - 3, 0, -2):
        pair = parts(state)
        state = dot3(pair, joint[g], NT) + (dot3(parts(pushes[g + 1]), maps[g], NT) + pushes[g])
        behind_v[g] = dot3(pair, maps[g + 1], NT) + pushes[g + 1]
        behind_v[g - 1] = state

    ahead = parts(ahead_v[mine])
    wave = wave_ref[...] + dot3(ahead, (wave_top[...], wave_rest[...]))
    wave_out[...] = wave
    adj = adj_ref[...] + dot3(ahead, (ahead_top[...], ahead_rest[...]))
    adj = adj + dot3(parts(behind_v[mine]), (behind_top[...], behind_rest[...]))
    adj_out[...] = adj
    image = jnp.sum(wave * adj, axis=0, keepdims=True) * (1.0 / (shots * rhs))
    top, rest = parts(image)
    hit = hit_ref[...]
    out_rows = hit.shape[0]
    table = jnp.concatenate([hit * top, hit * rest], axis=0)
    packed = dot(table, pick_ref[...], NT)
    packed = packed[:out_rows] + packed[out_rows:]
    each = out_rows // fronts
    for g in range(fronts):
        for r in range(rhs):
            image_out[g * rhs + r] = packed[g * each : (g + 1) * each]


def table_kernel(fronts, slot, front_ref, map_ref, token_ref, hit_ref, pick_ref):
    del token_ref
    each = slot // LANES
    count = map_ref.shape[0]
    groups = count // fronts
    cells = map_ref[...]
    mine = (cells >> (MC_DEV.bit_length() - 1)) == front_ref[0]
    rank = rank_in_order(mine.astype(F32), fronts, groups, True).astype(jnp.int32)
    rank = jnp.where(mine, rank, -1)
    local = cells & (MC_DEV - 1)
    coarse = (local >> 7).astype(F32)
    fine = (local & (LANES - 1)).astype(F32)
    high = rank >> 7
    low = jnp.where(mine, rank & (LANES - 1), -1)
    for f in range(fronts):
        table, pick = [], []
        for j in range(f * groups, (f + 1) * groups):
            hit = hits(each, high[j : j + 1])
            table.append(
                jnp.concatenate(
                    [jnp.where(hit, coarse[j : j + 1], 0.0), jnp.where(hit, fine[j : j + 1], 0.0)], axis=0
                ).astype(BF16)
            )
            pick.append(as_ones(hits(LANES, low[j : j + 1])))
        found = dot(jnp.concatenate(table, axis=1), jnp.concatenate(pick, axis=1), NT).astype(jnp.int32)
        for j in range(each):
            lanes = slice((f * each + j) * LANES, (f * each + j + 1) * LANES)
            hit_ref[:, lanes] = as_ones(hits(MC_DEV // LANES, found[j : j + 1]))
            pick_ref[:, lanes] = as_ones(hits(LANES, found[each + j : each + j + 1]))


def gather_kernel(fronts, rhs, terms_ref, hit_ref, pick_ref, out_ref):
    each = terms_ref.shape[1]
    rows = []
    for g in range(fronts):
        terms = terms_ref[g * rhs]
        for r in range(1, rhs):
            terms = terms + terms_ref[g * rhs + r]
        rows += [terms[j : j + 1] for j in range(each)]
    top, rest = parts(jnp.concatenate(rows, axis=1))
    hit = hit_ref[...]
    out_rows = hit.shape[0]
    found = dot(jnp.concatenate([hit * top, hit * rest], axis=0), pick_ref[...], NT)
    out_ref[...] = found[:out_rows] + found[out_rows:]


def body(signs, sources, dinv, u_fac, v_fac, ranks, dobs, cellmap):
    shots = signs.shape[0]
    blocks, width, n = u_fac.shape
    rows = blocks * width
    fronts = lax.axis_size("front")
    rhs = lax.axis_size("rhs")
    cap = 2 * rows // fronts
    slot = (cap + LANES - 1) // LANES * LANES
    each = slot // LANES
    groups = rows // LANES
    front = lax.axis_index("front").astype(jnp.int32).reshape(1)
    ut = jnp.swapaxes(u_fac, 1, 2)
    vt = jnp.swapaxes(v_fac, 1, 2)
    cells = cellmap.reshape(-1, LANES)
    middle = np.repeat(np.arange(n, dtype=np.float32)[:, None] + 0.5, width, axis=1)
    following = from_behind(jnp.where(middle < ranks[0].astype(F32), vt[0], 0.0), "front", -1)

    smem = pl.BlockSpec(memory_space=pltpu.SMEM)
    vmem = pl.BlockSpec(memory_space=pltpu.VMEM)
    hbm = pl.BlockSpec(memory_space=pltpu.HBM)

    def held(*arrays):
        return [pltpu.with_memory_space_constraint(a, pltpu.VMEM) for a in arrays]

    def far(*arrays):
        return [pltpu.with_memory_space_constraint(a, pltpu.HBM) for a in arrays]

    def cost(us):
        return pl.CostEstimate(flops=int(us * 1e9), bytes_accessed=int(us * 3e6), transcendentals=0)

    room = pltpu.CompilerParams(vmem_limit_bytes=24 * 2**20)

    y, maps, back = pl.pallas_call(
        prep_kernel,
        name="prep",
        out_shape=(
            pltpu.VMEM((blocks, shots + n, width), F32),
            pltpu.VMEM((blocks, shots + n, 4 * n), F32),
            pltpu.VMEM((shots + n, n), F32),
        ),
        in_specs=[hbm] * 7,
        out_specs=[vmem] * 3,
        scratch_shapes=[
            pltpu.SMEM(ranks.shape, ranks.dtype),
            pltpu.VMEM(signs.shape, signs.dtype),
            pltpu.VMEM(sources.shape, sources.dtype),
            pltpu.VMEM(dinv.shape, dinv.dtype),
            pltpu.VMEM(ut.shape, ut.dtype),
            pltpu.VMEM(vt.shape, vt.dtype),
            pltpu.VMEM(dobs.shape, dobs.dtype),
            pltpu.SemaphoreType.DMA((5,)),
            pltpu.SemaphoreType.DMA((2, blocks)),
        ],
        cost_estimate=cost(6),
        compiler_params=room,
    )(*far(ranks, signs, sources, dinv, ut, vt, dobs))

    send, last = pl.pallas_call(
        functools.partial(send_kernel, fronts),
        name="send",
        out_shape=(pltpu.VMEM((fronts, n, 4 * n), F32), pltpu.VMEM((n, n), F32)),
        in_specs=[vmem] * 4,
        out_specs=[vmem] * 2,
        cost_estimate=cost(0.5),
            )(*held(y, maps, following, back))

    got = lax.all_to_all(send, "front", 0, 0)

    fields = pl.pallas_call(
        functools.partial(fields_kernel, fronts, slot),
        name="fields",
        out_shape=(
            pltpu.VMEM((shots, rows), F32),
            pltpu.VMEM((n, rows), BF16),
            pltpu.VMEM((n, rows), BF16),
            pltpu.VMEM((shots, rows), F32),
            pltpu.VMEM((n, rows), BF16),
            pltpu.VMEM((n, rows), BF16),
            pltpu.VMEM((n, rows), BF16),
            pltpu.VMEM((n, rows), BF16),
            pltpu.VMEM((fronts * each, rows), BF16),
            pltpu.VMEM((LANES, rows), BF16),
        ),
        in_specs=[smem] + [vmem] * 4 + [hbm] * 5,
        out_specs=[vmem] * 10,
        scratch_shapes=[
            pltpu.VMEM((groups, LANES), cells.dtype),
            pltpu.VMEM(dinv.shape, dinv.dtype),
            pltpu.VMEM(vt.shape, vt.dtype),
            pltpu.VMEM(dobs.shape, dobs.dtype),
            pltpu.SMEM(ranks.shape, ranks.dtype),
            pltpu.SemaphoreType.DMA((4,)),
            pltpu.SemaphoreType.DMA((blocks,)),
        ],
        cost_estimate=cost(5),
        compiler_params=room,
    )(front, *held(y, maps, following, last), *far(cells, dinv, vt, dobs, ranks))

    wave, adj, image, token = pl.pallas_call(
        functools.partial(solve_kernel, fronts, rhs),
        name="solve",
        out_shape=(
            pltpu.VMEM((shots, rows), F32),
            pltpu.VMEM((shots, rows), F32),
            pltpu.VMEM((fronts * rhs, each, LANES), F32),
            pltpu.VMEM((8, LANES), F32),
        ),
        in_specs=[smem] + [vmem] * 11,
        out_specs=[vmem] * 4,
        scratch_shapes=[
            pltpu.VMEM((fronts, shots, n), F32),
            pltpu.VMEM((fronts, shots, n), F32),
        ],
        cost_estimate=cost(3),
        compiler_params=room,
    )(front, *held(got, *fields))

    terms = lax.all_to_all(image, ("front", "rhs"), 0, 0)

    hit, pick = pl.pallas_call(
        functools.partial(table_kernel, fronts, slot),
        name="tables",
        out_shape=(
            pltpu.VMEM((MC_DEV // LANES, fronts * slot), BF16),
            pltpu.VMEM((LANES, fronts * slot), BF16),
        ),
        in_specs=[smem, vmem, vmem],
        out_specs=[vmem] * 2,
        cost_estimate=cost(4),
        compiler_params=room,
    )(front, *far(cells), *held(token))

    gradient = pl.pallas_call(
        functools.partial(gather_kernel, fronts, rhs),
        name="gather",
        out_shape=jax.ShapeDtypeStruct((MC_DEV // LANES, LANES), F32),
        in_specs=[vmem] * 3,
        out_specs=vmem,
        cost_estimate=cost(1),
        compiler_params=room,
    )(*held(terms, hit, pick))
    return (wave, adj, gradient.reshape(MC_DEV))


def solution(mesh):
    in_specs = (
        P("rhs", None),
        P(None, "front"),
        P("front", None, None),
        P("front", None, None),
        P("front", None, None),
        P("front"),
        P("rhs", "front"),
        P(),
    )
    out_specs = (P("rhs", "front"), P("rhs", "front"), P("front"))
    return jax.shard_map(body, mesh=mesh, in_specs=in_specs, out_specs=out_specs, check_vma=False)
```

```python
import functools

import jax
import jax.numpy as jnp
import numpy as np
from jax import lax
from jax.experimental import pallas as pl
from jax.experimental.pallas import tpu as pltpu
from jax.sharding import PartitionSpec as P

MC_DEV = 8192
LANES = 128
F32 = jnp.float32
BF16 = jnp.bfloat16
NN = (((1,), (0,)), ((), ()))
NT = (((1,), (1,)), ((), ()))


def dot(a, b, dims=NN):
    return lax.dot_general(a, b, dims, preferred_element_type=F32)


def parts(x):
    top = x.astype(BF16)
    return top, (x - top.astype(F32)).astype(BF16)


def dot3(a, b, dims=NN):
    rows = a[0].shape[0]
    first = dot(jnp.concatenate(a, axis=0), b[0], dims)
    return first[:rows] + first[rows:] + dot(a[0], b[1], dims)


def rows_of(pair, start, stop):
    return pair[0][start:stop], pair[1][start:stop]


def hits(count, index):
    return lax.broadcasted_iota(jnp.int32, (count, LANES), 0) == index


def as_ones(mask):
    return mask.astype(F32).astype(BF16)


def from_behind(array, axis, by):
    length = lax.axis_size(axis)
    return lax.ppermute(array, axis, [(i, (i + by) % length) for i in range(length)])


def prep_kernel(
    ranks_hbm, signs_hbm, sources_hbm, dinv_hbm, ut_hbm, vt_hbm, dobs_hbm,
    y_ref, maps_ref, back_ref,
    ranks_ref, signs_v, sources_v, dinv_v, ut_v, vt_v, dobs_v, small_sem, block_sem,
):
    blocks, rank_max, width = ut_v.shape
    shots = signs_v.shape[0]
    small = [
        pltpu.make_async_copy(signs_hbm, signs_v, small_sem.at[0]),
        pltpu.make_async_copy(ut_hbm, ut_v, small_sem.at[1]),
        pltpu.make_async_copy(vt_hbm, vt_v, small_sem.at[2]),
        pltpu.make_async_copy(dobs_hbm, dobs_v, small_sem.at[3]),
        pltpu.make_async_copy(ranks_hbm, ranks_ref, small_sem.at[4]),
    ]
    large = []
    for k in range(blocks):
        columns = pl.ds(k * width, width)
        large.append(
            [
                pltpu.make_async_copy(sources_hbm.at[:, columns], sources_v.at[:, columns], block_sem.at[0, k]),
                pltpu.make_async_copy(dinv_hbm.at[k], dinv_v.at[k], block_sem.at[1, k]),
            ]
        )
    early = small[:1] + [pair[0] for pair in large]
    late = small[1:] + [pair[1] for pair in large]
    for copy in early + late:
        copy.start()
    for copy in early:
        copy.wait()

    sign = signs_v[...].astype(F32).astype(BF16)
    rank_row = lax.broadcasted_iota(jnp.int32, (rank_max, width), 0)
    products = {}
    for k in range(blocks):
        y_ref[k, :shots] = dot(sign, sources_v[:, k * width : (k + 1) * width])
    for copy in late:
        copy.wait()

    def sweep(k):
        left = jnp.where(rank_row < ranks_ref[k], ut_v[k], 0.0)
        y_ref[k] = dot3(parts(jnp.concatenate([y_ref[k, :shots], left], axis=0)), parts(dinv_v[k]), NT)

    def project(k):
        swept = y_ref[k]
        residual = parts(swept[:shots] - dobs_v[:, k * width : (k + 1) * width].astype(F32))
        swept = parts(swept)
        wave, ld = rows_of(swept, 0, shots), rows_of(swept, shots, None)
        if k + 1 < blocks:
            right = parts(jnp.where(rank_row < ranks_ref[k + 1], vt_v[k + 1], 0.0))
        else:
            right = parts(jnp.zeros((rank_max, width), F32))
        rows = tuple(jnp.concatenate(three, axis=0) for three in zip(wave, residual, ld))
        products[k] = dot3(rows, tuple(jnp.concatenate(two, axis=0) for two in zip(right, ld)), NT)

    for k in range(blocks):
        sweep(k)
    for k in range(blocks):
        project(k)

    n = rank_max
    nothing = jnp.zeros((n, n), F32)
    gains = [products[k][:shots, :n] for k in range(blocks)]
    fills = [products[k][shots : 2 * shots, n:] for k in range(blocks)]
    boths = [products[k][2 * shots :] for k in range(blocks)]

    def over(upper, product):
        return jnp.concatenate([upper - product[:shots], -product[shots:]], axis=0)

    joint = {}
    for k in range(1, blocks - 2, 2):
        follow = jnp.concatenate([gains[k], -boths[k][:, :n]], axis=0)
        joint[k] = over(gains[k + 1], dot3(parts(follow), parts(boths[k + 1][:, :n])))
    states = [None] * blocks
    states[1] = jnp.concatenate([gains[0], -boths[0][:, :n]], axis=0)
    pushes = [jnp.concatenate([fills[0], -boths[0][:, n:]], axis=0)] + [None] * (blocks - 1)
    for k in range(1, blocks):
        weights = [boths[k]]
        if k in joint:
            weights.append(-joint[k][shots:])
        after = dot3(parts(states[k]), parts(jnp.concatenate(weights, axis=1)))
        pushes[k] = over(fills[k], after[:, n : 2 * n])
        if k % 2 and k + 1 < blocks:
            states[k + 1] = over(gains[k], after[:, :n])
        if k in joint:
            states[k + 2] = over(joint[k][:shots], after[:, 2 * n :])
    long = jnp.concatenate(pushes[1:], axis=1)
    back = pushes[0] + dot3(parts(long), parts(jnp.concatenate([state[shots:] for state in states[1:]], axis=1)), NT)
    for k in range(blocks):
        if k + 1 < blocks:
            maps_ref[k, :, :n] = states[k + 1]
        maps_ref[k, :, n : 2 * n] = pushes[k]
        maps_ref[k, :n, 2 * n :] = boths[k]
    back_ref[...] = back


def send_kernel(fronts, y_ref, maps_ref, next_ref, back_ref, send_ref, last_ref):
    blocks = y_ref.shape[0]
    shots = y_ref.shape[1] - next_ref.shape[0]
    passed = dot3(parts(y_ref[blocks - 1]), parts(next_ref[...]), NT)
    forward = -passed[shots:]
    last_ref[...] = forward
    state = dot3(parts(maps_ref[blocks - 2, :, : forward.shape[0]]), parts(forward))
    back = back_ref[...]
    payload = jnp.concatenate(
        [state[shots:], state[:shots] + passed[:shots], back[shots:], back[:shots]], axis=1
    )
    for g in range(fronts):
        send_ref[g] = payload


def fields_kernel(
    fronts, slot, front_ref, y_ref, maps_ref, next_ref, last_ref, map_hbm, dinv_hbm, vt_hbm, dobs_hbm, ranks_hbm,
    wave_ref, wave_top, wave_rest, adj_ref, ahead_top, ahead_rest, behind_top, behind_rest, hit_ref, pick_ref, mine_ref,
    map_v, dinv_v, vt_v, dobs_v, ranks_ref, sem, block_sem,
):
    blocks, n, width = vt_v.shape
    shots = dobs_v.shape[0]
    groups = map_v.shape[0]
    start = pl.multiple_of(front_ref[0] * groups, groups)
    mine_ref[...] = (lax.broadcasted_iota(jnp.int32, mine_ref.shape, 0) == front_ref[0]).astype(F32)
    fetch = [
        pltpu.make_async_copy(vt_hbm, vt_v, sem.at[0]),
        pltpu.make_async_copy(dobs_hbm, dobs_v, sem.at[1]),
        pltpu.make_async_copy(ranks_hbm, ranks_ref, sem.at[2]),
        pltpu.make_async_copy(map_hbm.at[pl.ds(start, groups)], map_v, sem.at[3]),
    ]
    for copy in fetch:
        copy.start()
    large = [pltpu.make_async_copy(dinv_hbm.at[k], dinv_v.at[k], block_sem.at[k]) for k in range(blocks)]
    for copy in large:
        copy.start()

    unit_row = lax.broadcasted_iota(jnp.int32, (n, n), 0)
    unit_lane = lax.broadcasted_iota(jnp.int32, (n, n), 1)
    unit = (unit_row == unit_lane).astype(F32)
    nothing = jnp.zeros((n, n), F32)
    state = jnp.concatenate([jnp.zeros((shots + n, n), F32), unit], axis=0)
    backs = [None] * blocks
    for k in range(blocks - 1, 0, -1):
        backs[k] = state
        factor = parts(last_ref[...] if k + 1 == blocks else -maps_ref[k, :n, 2 * n : 3 * n])
        state = dot3(parts(state), factor, NT) + jnp.concatenate([maps_ref[k, :, n : 2 * n], nothing], axis=0)
    backs[0] = state
    for copy in fetch:
        copy.wait()

    owner = map_v[...] >> (MC_DEV.bit_length() - 1)
    member = jnp.concatenate([hits(fronts, owner[j : j + 1]).astype(F32) for j in range(groups)], axis=0)
    ranked = member * rank_in_order(member, fronts, groups, False)
    place = jnp.concatenate(
        [jnp.sum(ranked[j * fronts : (j + 1) * fronts], axis=0, keepdims=True) for j in range(groups)], axis=0
    ).astype(jnp.int32) + owner * slot
    out_rows = hit_ref.shape[0]
    for j in range(groups):
        lanes = slice(j * LANES, (j + 1) * LANES)
        at = place[j : j + 1]
        hit_ref[:, lanes] = as_ones(hits(out_rows, at >> 7))
        pick_ref[:, lanes] = as_ones(hits(LANES, at & (LANES - 1)))

    for copy in large:
        copy.wait()
    rank_row = lax.broadcasted_iota(jnp.int32, (n, width), 0)

    for k in range(blocks):
        columns = slice(k * width, (k + 1) * width)
        if k + 1 < blocks:
            right = jnp.where(rank_row < ranks_ref[k + 1], vt_v[k + 1], 0.0)
        else:
            right = next_ref[...]
        residual = y_ref[k, :shots] - dobs_v[:, columns].astype(F32)
        rows = jnp.concatenate([residual, y_ref[k, shots:], right], axis=0)
        returned = dot3(parts(rows), parts(dinv_v[k]))
        if k > 0:
            ahead = maps_ref[k - 1, :, :n]
        else:
            ahead = jnp.concatenate([jnp.zeros((shots, n), F32), unit], axis=0)
        wave = dot3(parts(ahead), parts(y_ref[k, shots:]))
        wave_ref[:, columns] = y_ref[k, :shots] - wave[:shots]
        wave_top[:, columns], wave_rest[:, columns] = parts(-wave[shots:])
        enters = jnp.concatenate([jnp.concatenate([ahead, nothing], axis=0), backs[k]], axis=1)
        adj = dot3(parts(enters), parts(returned[shots:]))
        adj_ref[:, columns] = returned[:shots] - adj[:shots]
        ahead_top[:, columns], ahead_rest[:, columns] = parts(-adj[shots : shots + n])
        behind_top[:, columns], behind_rest[:, columns] = parts(-adj[shots + n :])


def rank_in_order(member, stride, groups, blocked):
    count = member.shape[0]
    row = lax.broadcasted_iota(jnp.int32, (LANES, LANES), 0)
    lane = lax.broadcasted_iota(jnp.int32, (LANES, LANES), 1)
    member = member.astype(BF16)
    inside = dot(member, as_ones(row < lane))
    total = dot(member, jnp.ones((LANES, LANES), BF16))
    p = lax.broadcasted_iota(jnp.int32, (count, count), 0)
    q = lax.broadcasted_iota(jnp.int32, (count, count), 1)
    if blocked:
        shift = groups.bit_length() - 1
        same = (p >> shift) == (q >> shift)
    else:
        same = (p & (stride - 1)) == (q & (stride - 1))
    return inside + dot(as_ones(same & (q < p)), total.astype(BF16))


def solve_kernel(
    fronts, rhs, got_ref, wave_ref, wave_top, wave_rest, adj_ref, ahead_top, ahead_rest,
    behind_top, behind_rest, hit_ref, pick_ref, mine_ref,
    wave_out, adj_out, image_out, token_ref,
):
    shots, rows = wave_ref.shape
    n = wave_top.shape[0]
    token_ref[...] = jnp.zeros_like(token_ref)
    ahead_v, behind_v = {}, {}
    zero = jnp.zeros((shots, n), F32)

    maps = [parts(got_ref[g, :, :n]) for g in range(fronts)]
    gains = [got_ref[g, :, n : 2 * n] for g in range(fronts)]
    joint = {g: parts(dot3(maps[g], maps[g + 1])) for g in range(1, fronts - 1, 2)}
    ahead_v[0] = zero
    ahead_v[1] = gains[0]
    state = gains[0]
    pushes = [None] * fronts

    def push(g, pair):
        pushes[g] = dot3(pair, parts(got_ref[g, :, 2 * n : 3 * n])) + got_ref[g, :, 3 * n :]

    for g in range(1, fronts - 1, 2):
        pair = parts(state)
        state = dot3(pair, joint[g]) + (dot3(parts(gains[g]), maps[g + 1]) + gains[g + 1])
        push(g, pair)
        between = dot3(pair, maps[g]) + gains[g]
        ahead_v[g + 1] = between
        push(g + 1, parts(between))
        ahead_v[g + 2] = state
    push(fronts - 1, parts(state))
    behind_v[fronts - 1] = zero
    state = pushes[fronts - 1]
    behind_v[fronts - 2] = state
    for g in range(fronts - 3, 0, -2):
        pair = parts(state)
        state = dot3(pair, joint[g], NT) + (dot3(parts(pushes[g + 1]), maps[g], NT) + pushes[g])
        behind_v[g] = dot3(pair, maps[g + 1], NT) + pushes[g + 1]
        behind_v[g - 1] = state

    def own(choices):
        value = choices[0]
        for g in range(1, fronts):
            value = jnp.where(mine_ref[g : g + 1, :n] > 0.5, choices[g], value)
        return parts(value)

    ahead = own(ahead_v)
    wave = wave_ref[...] + dot3(ahead, (wave_top[...], wave_rest[...]))
    wave_out[...] = wave
    adj = adj_ref[...] + dot3(ahead, (ahead_top[...], ahead_rest[...]))
    adj = adj + dot3(own(behind_v), (behind_top[...], behind_rest[...]))
    adj_out[...] = adj
    image = jnp.sum(wave * adj, axis=0, keepdims=True) * (1.0 / (shots * rhs))
    top, rest = parts(image)
    hit = hit_ref[...]
    out_rows = hit.shape[0]
    table = jnp.concatenate([hit * top, hit * rest], axis=0)
    packed = dot(table, pick_ref[...], NT)
    packed = packed[:out_rows] + packed[out_rows:]
    each = out_rows // fronts
    for g in range(fronts):
        for r in range(rhs):
            image_out[g * rhs + r] = packed[g * each : (g + 1) * each]


def table_kernel(fronts, slot, front_ref, map_ref, token_ref, hit_ref, pick_ref):
    del token_ref
    each = slot // LANES
    count = map_ref.shape[0]
    groups = count // fronts
    cells = map_ref[...]
    mine = (cells >> (MC_DEV.bit_length() - 1)) == front_ref[0]
    rank = rank_in_order(mine.astype(F32), fronts, groups, True).astype(jnp.int32)
    rank = jnp.where(mine, rank, -1)
    local = cells & (MC_DEV - 1)
    coarse = (local >> 7).astype(F32)
    fine = (local & (LANES - 1)).astype(F32)
    high = rank >> 7
    low = jnp.where(mine, rank & (LANES - 1), -1)
    for f in range(fronts):
        table, pick = [], []
        for j in range(f * groups, (f + 1) * groups):
            hit = hits(each, high[j : j + 1])
            table.append(
                jnp.concatenate(
                    [jnp.where(hit, coarse[j : j + 1], 0.0), jnp.where(hit, fine[j : j + 1], 0.0)], axis=0
                ).astype(BF16)
            )
            pick.append(as_ones(hits(LANES, low[j : j + 1])))
        found = dot(jnp.concatenate(table, axis=1), jnp.concatenate(pick, axis=1), NT).astype(jnp.int32)
        for j in range(each):
            lanes = slice((f * each + j) * LANES, (f * each + j + 1) * LANES)
            hit_ref[:, lanes] = as_ones(hits(MC_DEV // LANES, found[j : j + 1]))
            pick_ref[:, lanes] = as_ones(hits(LANES, found[each + j : each + j + 1]))


def gather_kernel(fronts, rhs, terms_ref, hit_ref, pick_ref, out_ref):
    each = terms_ref.shape[1]
    rows = []
    for g in range(fronts):
        terms = terms_ref[g * rhs]
        for r in range(1, rhs):
            terms = terms + terms_ref[g * rhs + r]
        rows += [terms[j : j + 1] for j in range(each)]
    top, rest = parts(jnp.concatenate(rows, axis=1))
    hit = hit_ref[...]
    out_rows = hit.shape[0]
    found = dot(jnp.concatenate([hit * top, hit * rest], axis=0), pick_ref[...], NT)
    out_ref[...] = found[:out_rows] + found[out_rows:]


def body(signs, sources, dinv, u_fac, v_fac, ranks, dobs, cellmap):
    shots = signs.shape[0]
    blocks, width, n = u_fac.shape
    rows = blocks * width
    fronts = lax.axis_size("front")
    rhs = lax.axis_size("rhs")
    cap = 2 * rows // fronts
    slot = (cap + LANES - 1) // LANES * LANES
    each = slot // LANES
    groups = rows // LANES
    front = lax.axis_index("front").astype(jnp.int32).reshape(1)
    ut = jnp.swapaxes(u_fac, 1, 2)
    vt = jnp.swapaxes(v_fac, 1, 2)
    cells = cellmap.reshape(-1, LANES)
    middle = np.repeat(np.arange(n, dtype=np.float32)[:, None] + 0.5, width, axis=1)
    alive = jnp.where(lax.axis_index("front") == 0, 0, ranks[0]).astype(F32)
    following = from_behind(jnp.where(middle < alive, vt[0], 0.0), "front", -1)

    smem = pl.BlockSpec(memory_space=pltpu.SMEM)
    vmem = pl.BlockSpec(memory_space=pltpu.VMEM)
    hbm = pl.BlockSpec(memory_space=pltpu.HBM)

    def held(*arrays):
        return [pltpu.with_memory_space_constraint(a, pltpu.VMEM) for a in arrays]

    def far(*arrays):
        return [pltpu.with_memory_space_constraint(a, pltpu.HBM) for a in arrays]

    def cost(us):
        return pl.CostEstimate(flops=int(us * 1e9), bytes_accessed=int(us * 3e6), transcendentals=0)

    room = pltpu.CompilerParams(vmem_limit_bytes=24 * 2**20)

    y, maps, back = pl.pallas_call(
        prep_kernel,
        name="prep",
        out_shape=(
            pltpu.VMEM((blocks, shots + n, width), F32),
            pltpu.VMEM((blocks, shots + n, 4 * n), F32),
            pltpu.VMEM((shots + n, n), F32),
        ),
        in_specs=[hbm] * 7,
        out_specs=[vmem] * 3,
        scratch_shapes=[
            pltpu.SMEM(ranks.shape, ranks.dtype),
            pltpu.VMEM(signs.shape, signs.dtype),
            pltpu.VMEM(sources.shape, sources.dtype),
            pltpu.VMEM(dinv.shape, dinv.dtype),
            pltpu.VMEM(ut.shape, ut.dtype),
            pltpu.VMEM(vt.shape, vt.dtype),
            pltpu.VMEM(dobs.shape, dobs.dtype),
            pltpu.SemaphoreType.DMA((5,)),
            pltpu.SemaphoreType.DMA((2, blocks)),
        ],
        cost_estimate=cost(6),
        compiler_params=room,
    )(*far(ranks, signs, sources, dinv, ut, vt, dobs))

    send, last = pl.pallas_call(
        functools.partial(send_kernel, fronts),
        name="send",
        out_shape=(pltpu.VMEM((fronts, n, 4 * n), F32), pltpu.VMEM((n, n), F32)),
        in_specs=[vmem] * 4,
        out_specs=[vmem] * 2,
        cost_estimate=cost(0.5),
            )(*held(y, maps, following, back))

    got = lax.all_to_all(send, "front", 0, 0)

    fields = pl.pallas_call(
        functools.partial(fields_kernel, fronts, slot),
        name="fields",
        out_shape=(
            pltpu.VMEM((shots, rows), F32),
            pltpu.VMEM((n, rows), BF16),
            pltpu.VMEM((n, rows), BF16),
            pltpu.VMEM((shots, rows), F32),
            pltpu.VMEM((n, rows), BF16),
            pltpu.VMEM((n, rows), BF16),
            pltpu.VMEM((n, rows), BF16),
            pltpu.VMEM((n, rows), BF16),
            pltpu.VMEM((fronts * each, rows), BF16),
            pltpu.VMEM((LANES, rows), BF16),
            pltpu.VMEM((fronts, LANES), F32),
        ),
        in_specs=[smem] + [vmem] * 4 + [hbm] * 5,
        out_specs=[vmem] * 11,
        scratch_shapes=[
            pltpu.VMEM((groups, LANES), cells.dtype),
            pltpu.VMEM(dinv.shape, dinv.dtype),
            pltpu.VMEM(vt.shape, vt.dtype),
            pltpu.VMEM(dobs.shape, dobs.dtype),
            pltpu.SMEM(ranks.shape, ranks.dtype),
            pltpu.SemaphoreType.DMA((4,)),
            pltpu.SemaphoreType.DMA((blocks,)),
        ],
        cost_estimate=cost(5),
        compiler_params=room,
    )(front, *held(y, maps, following, last), *far(cells, dinv, vt, dobs, ranks))

    wave, adj, image, token = pl.pallas_call(
        functools.partial(solve_kernel, fronts, rhs),
        name="solve",
        out_shape=(
            pltpu.VMEM((shots, rows), F32),
            pltpu.VMEM((shots, rows), F32),
            pltpu.VMEM((fronts * rhs, each, LANES), F32),
            pltpu.VMEM((8, LANES), F32),
        ),
        in_specs=[vmem] * 12,
        out_specs=[vmem] * 4,
        cost_estimate=cost(3),
        compiler_params=room,
    )(*held(got, *fields))

    terms = lax.all_to_all(image, ("front", "rhs"), 0, 0)

    hit, pick = pl.pallas_call(
        functools.partial(table_kernel, fronts, slot),
        name="tables",
        out_shape=(
            pltpu.VMEM((MC_DEV // LANES, fronts * slot), BF16),
            pltpu.VMEM((LANES, fronts * slot), BF16),
        ),
        in_specs=[smem, vmem, vmem],
        out_specs=[vmem] * 2,
        cost_estimate=cost(4),
        compiler_params=room,
    )(front, *far(cells), *held(token))

    gradient = pl.pallas_call(
        functools.partial(gather_kernel, fronts, rhs),
        name="gather",
        out_shape=jax.ShapeDtypeStruct((MC_DEV // LANES, LANES), F32),
        in_specs=[vmem] * 3,
        out_specs=vmem,
        cost_estimate=cost(1),
        compiler_params=room,
    )(*held(terms, hit, pick))
    return (wave, adj, gradient.reshape(MC_DEV))


def solution(mesh):
    in_specs = (
        P("rhs", None),
        P(None, "front"),
        P("front", None, None),
        P("front", None, None),
        P("front", None, None),
        P("front"),
        P("rhs", "front"),
        P(),
    )
    out_specs = (P("rhs", "front"), P("rhs", "front"), P("front"))
    return jax.shard_map(body, mesh=mesh, in_specs=in_specs, out_specs=out_specs, check_vma=False)
```

```python
import functools

import jax
import jax.numpy as jnp
import numpy as np
from jax import lax
from jax.experimental import pallas as pl
from jax.experimental.pallas import tpu as pltpu
from jax.sharding import PartitionSpec as P

MC_DEV = 8192
LANES = 128
F32 = jnp.float32
BF16 = jnp.bfloat16
NN = (((1,), (0,)), ((), ()))
NT = (((1,), (1,)), ((), ()))


def dot(a, b, dims=NN):
    return lax.dot_general(a, b, dims, preferred_element_type=F32)


def parts(x):
    top = x.astype(BF16)
    return top, (x - top.astype(F32)).astype(BF16)


def dot3(a, b, dims=NN):
    rows = a[0].shape[0]
    first = dot(jnp.concatenate(a, axis=0), b[0], dims)
    return first[:rows] + first[rows:] + dot(a[0], b[1], dims)


def rows_of(pair, start, stop):
    return pair[0][start:stop], pair[1][start:stop]


def hits(count, index):
    return lax.broadcasted_iota(jnp.int32, (count, LANES), 0) == index


def as_ones(mask):
    return mask.astype(F32).astype(BF16)


def from_behind(array, axis, by):
    length = lax.axis_size(axis)
    return lax.ppermute(array, axis, [(i, (i + by) % length) for i in range(length)])


def prep_kernel(
    ranks_hbm, signs_hbm, sources_hbm, dinv_hbm, ut_hbm, vt_hbm, dobs_hbm,
    y_ref, maps_ref, back_ref,
    ranks_ref, signs_v, sources_v, dinv_v, ut_v, vt_v, dobs_v, small_sem, block_sem,
):
    blocks, rank_max, width = ut_v.shape
    shots = signs_v.shape[0]
    small = [
        pltpu.make_async_copy(signs_hbm, signs_v, small_sem.at[0]),
        pltpu.make_async_copy(ut_hbm, ut_v, small_sem.at[1]),
        pltpu.make_async_copy(vt_hbm, vt_v, small_sem.at[2]),
        pltpu.make_async_copy(dobs_hbm, dobs_v, small_sem.at[3]),
        pltpu.make_async_copy(ranks_hbm, ranks_ref, small_sem.at[4]),
    ]
    large = []
    for k in range(blocks):
        columns = pl.ds(k * width, width)
        large.append(
            [
                pltpu.make_async_copy(sources_hbm.at[:, columns], sources_v.at[:, columns], block_sem.at[0, k]),
                pltpu.make_async_copy(dinv_hbm.at[k], dinv_v.at[k], block_sem.at[1, k]),
            ]
        )
    early = small[:1] + [pair[0] for pair in large]
    late = small[1:] + [pair[1] for pair in large]
    for copy in early + late:
        copy.start()
    for copy in early:
        copy.wait()

    sign = signs_v[...].astype(F32).astype(BF16)
    rank_row = lax.broadcasted_iota(jnp.int32, (rank_max, width), 0)
    products = {}
    for k in range(blocks):
        y_ref[k, :shots] = dot(sign, sources_v[:, k * width : (k + 1) * width])
    for copy in late:
        copy.wait()

    def sweep(k):
        left = jnp.where(rank_row < ranks_ref[k], ut_v[k], 0.0)
        y_ref[k] = dot3(parts(jnp.concatenate([y_ref[k, :shots], left], axis=0)), parts(dinv_v[k]), NT)

    def project(k):
        swept = y_ref[k]
        residual = parts(swept[:shots] - dobs_v[:, k * width : (k + 1) * width].astype(F32))
        swept = parts(swept)
        wave, ld = rows_of(swept, 0, shots), rows_of(swept, shots, None)
        if k + 1 < blocks:
            right = parts(jnp.where(rank_row < ranks_ref[k + 1], vt_v[k + 1], 0.0))
        else:
            right = parts(jnp.zeros((rank_max, width), F32))
        rows = tuple(jnp.concatenate(three, axis=0) for three in zip(wave, residual, ld))
        products[k] = dot3(rows, tuple(jnp.concatenate(two, axis=0) for two in zip(right, ld)), NT)

    for k in range(blocks):
        sweep(k)
    for k in range(blocks):
        project(k)

    n = rank_max
    nothing = jnp.zeros((n, n), F32)
    gains = [products[k][:shots, :n] for k in range(blocks)]
    fills = [products[k][shots : 2 * shots, n:] for k in range(blocks)]
    boths = [products[k][2 * shots :] for k in range(blocks)]

    def over(upper, product):
        return jnp.concatenate([upper - product[:shots], -product[shots:]], axis=0)

    joint = {}
    for k in range(1, blocks - 2, 2):
        follow = jnp.concatenate([gains[k], -boths[k][:, :n]], axis=0)
        joint[k] = over(gains[k + 1], dot3(parts(follow), parts(boths[k + 1][:, :n])))
    states = [None] * blocks
    states[1] = jnp.concatenate([gains[0], -boths[0][:, :n]], axis=0)
    pushes = [jnp.concatenate([fills[0], -boths[0][:, n:]], axis=0)] + [None] * (blocks - 1)
    for k in range(1, blocks):
        weights = [boths[k]]
        if k in joint:
            weights.append(-joint[k][shots:])
        after = dot3(parts(states[k]), parts(jnp.concatenate(weights, axis=1)))
        pushes[k] = over(fills[k], after[:, n : 2 * n])
        if k % 2 and k + 1 < blocks:
            states[k + 1] = over(gains[k], after[:, :n])
        if k in joint:
            states[k + 2] = over(joint[k][:shots], after[:, 2 * n :])
    long = jnp.concatenate(pushes[1:], axis=1)
    back = pushes[0] + dot3(parts(long), parts(jnp.concatenate([state[shots:] for state in states[1:]], axis=1)), NT)
    for k in range(blocks):
        if k + 1 < blocks:
            maps_ref[k, :, :n] = states[k + 1]
        maps_ref[k, :, n : 2 * n] = pushes[k]
        maps_ref[k, :n, 2 * n :] = boths[k]
    back_ref[...] = back


def send_kernel(fronts, y_ref, maps_ref, next_ref, back_ref, send_ref, last_ref):
    blocks = y_ref.shape[0]
    shots = y_ref.shape[1] - next_ref.shape[0]
    passed = dot3(parts(y_ref[blocks - 1]), parts(next_ref[...]), NT)
    forward = -passed[shots:]
    last_ref[...] = forward
    state = dot3(parts(maps_ref[blocks - 2, :, : forward.shape[0]]), parts(forward))
    back = back_ref[...]
    payload = jnp.concatenate(
        [state[shots:], state[:shots] + passed[:shots], back[shots:], back[:shots]], axis=1
    )
    for g in range(fronts):
        send_ref[g] = payload


def fields_kernel(
    fronts, slot, front_ref, y_ref, maps_ref, next_ref, last_ref, map_hbm, dinv_hbm, vt_hbm, dobs_hbm, ranks_hbm,
    wave_ref, wave_top, wave_rest, adj_ref, ahead_top, ahead_rest, behind_top, behind_rest, hit_ref, pick_ref, mine_ref,
    map_v, dinv_v, vt_v, dobs_v, ranks_ref, sem, block_sem,
):
    blocks, n, width = vt_v.shape
    shots = dobs_v.shape[0]
    groups = map_v.shape[0]
    start = pl.multiple_of(front_ref[0] * groups, groups)
    mine_ref[...] = (lax.broadcasted_iota(jnp.int32, mine_ref.shape, 0) == front_ref[0]).astype(F32)
    fetch = [
        pltpu.make_async_copy(vt_hbm, vt_v, sem.at[0]),
        pltpu.make_async_copy(dobs_hbm, dobs_v, sem.at[1]),
        pltpu.make_async_copy(ranks_hbm, ranks_ref, sem.at[2]),
        pltpu.make_async_copy(map_hbm.at[pl.ds(start, groups)], map_v, sem.at[3]),
    ]
    for copy in fetch:
        copy.start()
    large = [pltpu.make_async_copy(dinv_hbm.at[k], dinv_v.at[k], block_sem.at[k]) for k in range(blocks)]
    for copy in large:
        copy.start()

    unit_row = lax.broadcasted_iota(jnp.int32, (n, n), 0)
    unit_lane = lax.broadcasted_iota(jnp.int32, (n, n), 1)
    unit = (unit_row == unit_lane).astype(F32)
    nothing = jnp.zeros((n, n), F32)
    state = jnp.concatenate([jnp.zeros((shots + n, n), F32), unit], axis=0)
    backs = [None] * blocks
    for k in range(blocks - 1, 0, -1):
        backs[k] = state
        factor = parts(last_ref[...] if k + 1 == blocks else -maps_ref[k, :n, 2 * n : 3 * n])
        state = dot3(parts(state), factor, NT) + jnp.concatenate([maps_ref[k, :, n : 2 * n], nothing], axis=0)
    backs[0] = state
    for copy in fetch:
        copy.wait()

    owner = map_v[...] >> (MC_DEV.bit_length() - 1)
    member = jnp.concatenate([hits(fronts, owner[j : j + 1]).astype(F32) for j in range(groups)], axis=0)
    ranked = member * rank_in_order(member, fronts, groups, False)
    place = jnp.concatenate(
        [jnp.sum(ranked[j * fronts : (j + 1) * fronts], axis=0, keepdims=True) for j in range(groups)], axis=0
    ).astype(jnp.int32) + owner * slot
    out_rows = hit_ref.shape[0]
    for j in range(groups):
        lanes = slice(j * LANES, (j + 1) * LANES)
        at = place[j : j + 1]
        hit_ref[:, lanes] = as_ones(hits(out_rows, at >> 7))
        pick_ref[:, lanes] = as_ones(hits(LANES, at & (LANES - 1)))

    for copy in large:
        copy.wait()
    rank_row = lax.broadcasted_iota(jnp.int32, (n, width), 0)

    for k in range(blocks):
        columns = slice(k * width, (k + 1) * width)
        if k + 1 < blocks:
            right = jnp.where(rank_row < ranks_ref[k + 1], vt_v[k + 1], 0.0)
        else:
            right = next_ref[...]
        residual = y_ref[k, :shots] - dobs_v[:, columns].astype(F32)
        rows = jnp.concatenate([residual, y_ref[k, shots:], right], axis=0)
        returned = dot3(parts(rows), parts(dinv_v[k]))
        if k > 0:
            ahead = maps_ref[k - 1, :, :n]
        else:
            ahead = jnp.concatenate([jnp.zeros((shots, n), F32), unit], axis=0)
        wave = dot3(parts(ahead), parts(y_ref[k, shots:]))
        wave_ref[:, columns] = y_ref[k, :shots] - wave[:shots]
        wave_top[:, columns], wave_rest[:, columns] = parts(-wave[shots:])
        enters = jnp.concatenate([jnp.concatenate([ahead, nothing], axis=0), backs[k]], axis=1)
        adj = dot3(parts(enters), parts(returned[shots:]))
        adj_ref[:, columns] = returned[:shots] - adj[:shots]
        ahead_top[:, columns], ahead_rest[:, columns] = parts(-adj[shots : shots + n])
        behind_top[:, columns], behind_rest[:, columns] = parts(-adj[shots + n :])


def rank_in_order(member, stride, groups, blocked):
    count = member.shape[0]
    row = lax.broadcasted_iota(jnp.int32, (LANES, LANES), 0)
    lane = lax.broadcasted_iota(jnp.int32, (LANES, LANES), 1)
    member = member.astype(BF16)
    inside = dot(member, as_ones(row < lane))
    total = dot(member, jnp.ones((LANES, LANES), BF16))
    p = lax.broadcasted_iota(jnp.int32, (count, count), 0)
    q = lax.broadcasted_iota(jnp.int32, (count, count), 1)
    if blocked:
        shift = groups.bit_length() - 1
        same = (p >> shift) == (q >> shift)
    else:
        same = (p & (stride - 1)) == (q & (stride - 1))
    return inside + dot(as_ones(same & (q < p)), total.astype(BF16))


def solve_kernel(
    fronts, rhs, got_ref, wave_ref, wave_top, wave_rest, adj_ref, ahead_top, ahead_rest,
    behind_top, behind_rest, hit_ref, pick_ref, mine_ref,
    wave_out, adj_out, image_out, token_ref,
):
    shots, rows = wave_ref.shape
    n = wave_top.shape[0]
    token_ref[...] = jnp.zeros_like(token_ref)
    ahead_v, behind_v = {}, {}
    zero = jnp.zeros((shots, n), F32)

    maps = [parts(got_ref[g, :, :n]) for g in range(fronts)]
    gains = [got_ref[g, :, n : 2 * n] for g in range(fronts)]
    joint = {g: parts(dot3(maps[g], maps[g + 1])) for g in range(1, fronts - 1, 2)}
    ahead_v[0] = zero
    ahead_v[1] = gains[0]
    state = gains[0]
    pushes = [None] * fronts

    def push(g, pair):
        pushes[g] = dot3(pair, parts(got_ref[g, :, 2 * n : 3 * n])) + got_ref[g, :, 3 * n :]

    for g in range(1, fronts - 1, 2):
        pair = parts(state)
        state = dot3(pair, joint[g]) + (dot3(parts(gains[g]), maps[g + 1]) + gains[g + 1])
        push(g, pair)
        between = dot3(pair, maps[g]) + gains[g]
        ahead_v[g + 1] = between
        push(g + 1, parts(between))
        ahead_v[g + 2] = state
    push(fronts - 1, parts(state))
    behind_v[fronts - 1] = zero
    state = pushes[fronts - 1]
    behind_v[fronts - 2] = state
    for g in range(fronts - 3, 0, -2):
        pair = parts(state)
        state = dot3(pair, joint[g], NT) + (dot3(parts(pushes[g + 1]), maps[g], NT) + pushes[g])
        behind_v[g] = dot3(pair, maps[g + 1], NT) + pushes[g + 1]
        behind_v[g - 1] = state

    def own(choices):
        value = choices[0]
        for g in range(1, fronts):
            value = jnp.where(mine_ref[g : g + 1, :n] > 0.5, choices[g], value)
        return parts(value)

    ahead = own(ahead_v)
    wave = wave_ref[...] + dot3(ahead, (wave_top[...], wave_rest[...]))
    wave_out[...] = wave
    adj = adj_ref[...] + dot3(ahead, (ahead_top[...], ahead_rest[...]))
    adj = adj + dot3(own(behind_v), (behind_top[...], behind_rest[...]))
    adj_out[...] = adj
    image = jnp.sum(wave * adj, axis=0, keepdims=True) * (1.0 / (shots * rhs))
    top, rest = parts(image)
    hit = hit_ref[...]
    out_rows = hit.shape[0]
    table = jnp.concatenate([hit * top, hit * rest], axis=0)
    packed = dot(table, pick_ref[...], NT)
    packed = packed[:out_rows] + packed[out_rows:]
    each = out_rows // fronts
    for g in range(fronts):
        for r in range(rhs):
            image_out[g * rhs + r] = packed[g * each : (g + 1) * each]


def table_kernel(fronts, slot, front_ref, map_ref, token_ref, hit_ref, pick_ref):
    del token_ref
    each = slot // LANES
    count = map_ref.shape[0]
    groups = count // fronts
    cells = map_ref[...]
    mine = (cells >> (MC_DEV.bit_length() - 1)) == front_ref[0]
    rank = rank_in_order(mine.astype(F32), fronts, groups, True).astype(jnp.int32)
    rank = jnp.where(mine, rank, -1)
    local = cells & (MC_DEV - 1)
    coarse = (local >> 7).astype(F32)
    fine = (local & (LANES - 1)).astype(F32)
    high = rank >> 7
    low = jnp.where(mine, rank & (LANES - 1), -1)
    for f in range(fronts):
        table, pick = [], []
        for j in range(f * groups, (f + 1) * groups):
            hit = hits(each, high[j : j + 1])
            table.append(
                jnp.concatenate(
                    [jnp.where(hit, coarse[j : j + 1], 0.0), jnp.where(hit, fine[j : j + 1], 0.0)], axis=0
                ).astype(BF16)
            )
            pick.append(as_ones(hits(LANES, low[j : j + 1])))
        found = dot(jnp.concatenate(table, axis=1), jnp.concatenate(pick, axis=1), NT).astype(jnp.int32)
        for j in range(each):
            lanes = slice((f * each + j) * LANES, (f * each + j + 1) * LANES)
            hit_ref[:, lanes] = as_ones(hits(MC_DEV // LANES, found[j : j + 1]))
            pick_ref[:, lanes] = as_ones(hits(LANES, found[each + j : each + j + 1]))


def gather_kernel(fronts, rhs, terms_ref, hit_ref, pick_ref, out_ref):
    each = terms_ref.shape[1]
    rows = []
    for g in range(fronts):
        terms = terms_ref[g * rhs]
        for r in range(1, rhs):
            terms = terms + terms_ref[g * rhs + r]
        rows += [terms[j : j + 1] for j in range(each)]
    top, rest = parts(jnp.concatenate(rows, axis=1))
    hit = hit_ref[...]
    out_rows = hit.shape[0]
    found = dot(jnp.concatenate([hit * top, hit * rest], axis=0), pick_ref[...], NT)
    out_ref[...] = found[:out_rows] + found[out_rows:]


def body(signs, sources, dinv, u_fac, v_fac, ranks, dobs, cellmap):
    shots = signs.shape[0]
    blocks, width, n = u_fac.shape
    rows = blocks * width
    fronts = lax.axis_size("front")
    rhs = lax.axis_size("rhs")
    cap = 2 * rows // fronts
    slot = (cap + LANES - 1) // LANES * LANES
    each = slot // LANES
    groups = rows // LANES
    front = lax.axis_index("front").astype(jnp.int32).reshape(1)
    ut = jnp.swapaxes(u_fac, 1, 2)
    vt = jnp.swapaxes(v_fac, 1, 2)
    cells = cellmap.reshape(-1, LANES)
    middle = np.repeat(np.arange(n, dtype=np.float32)[:, None] + 0.5, width, axis=1)
    alive = jnp.where(lax.axis_index("front") == 0, 0, ranks[0]).astype(F32)
    following = from_behind(jnp.where(middle < alive, vt[0], 0.0), "front", -1)

    smem = pl.BlockSpec(memory_space=pltpu.SMEM)
    vmem = pl.BlockSpec(memory_space=pltpu.VMEM)
    hbm = pl.BlockSpec(memory_space=pltpu.HBM)

    def held(*arrays):
        return [pltpu.with_memory_space_constraint(a, pltpu.VMEM) for a in arrays]

    def far(*arrays):
        return [pltpu.with_memory_space_constraint(a, pltpu.HBM) for a in arrays]

    def cost(us):
        return pl.CostEstimate(flops=int(us * 1e9), bytes_accessed=int(us * 3e6), transcendentals=0)

    room = pltpu.CompilerParams(vmem_limit_bytes=24 * 2**20)
    packed = pltpu.CompilerParams(vmem_limit_bytes=24 * 2**20)

    y, maps, back = pl.pallas_call(
        prep_kernel,
        name="prep",
        out_shape=(
            pltpu.VMEM((blocks, shots + n, width), F32),
            pltpu.VMEM((blocks, shots + n, 4 * n), F32),
            pltpu.VMEM((shots + n, n), F32),
        ),
        in_specs=[hbm] * 7,
        out_specs=[vmem] * 3,
        scratch_shapes=[
            pltpu.SMEM(ranks.shape, ranks.dtype),
            pltpu.VMEM(signs.shape, signs.dtype),
            pltpu.VMEM(sources.shape, sources.dtype),
            pltpu.VMEM(dinv.shape, dinv.dtype),
            pltpu.VMEM(ut.shape, ut.dtype),
            pltpu.VMEM(vt.shape, vt.dtype),
            pltpu.VMEM(dobs.shape, dobs.dtype),
            pltpu.SemaphoreType.DMA((5,)),
            pltpu.SemaphoreType.DMA((2, blocks)),
        ],
        cost_estimate=cost(6),
        compiler_params=packed,
    )(*far(ranks, signs, sources, dinv, ut, vt, dobs))

    send, last = pl.pallas_call(
        functools.partial(send_kernel, fronts),
        name="send",
        out_shape=(pltpu.VMEM((fronts, n, 4 * n), F32), pltpu.VMEM((n, n), F32)),
        in_specs=[vmem] * 4,
        out_specs=[vmem] * 2,
        cost_estimate=cost(0.5),
            )(*held(y, maps, following, back))

    got = lax.all_to_all(send, "front", 0, 0)

    fields = pl.pallas_call(
        functools.partial(fields_kernel, fronts, slot),
        name="fields",
        out_shape=(
            pltpu.VMEM((shots, rows), F32),
            pltpu.VMEM((n, rows), BF16),
            pltpu.VMEM((n, rows), BF16),
            pltpu.VMEM((shots, rows), F32),
            pltpu.VMEM((n, rows), BF16),
            pltpu.VMEM((n, rows), BF16),
            pltpu.VMEM((n, rows), BF16),
            pltpu.VMEM((n, rows), BF16),
            pltpu.VMEM((fronts * each, rows), BF16),
            pltpu.VMEM((LANES, rows), BF16),
            pltpu.VMEM((fronts, LANES), F32),
        ),
        in_specs=[smem] + [vmem] * 4 + [hbm] * 5,
        out_specs=[vmem] * 11,
        scratch_shapes=[
            pltpu.VMEM((groups, LANES), cells.dtype),
            pltpu.VMEM(dinv.shape, dinv.dtype),
            pltpu.VMEM(vt.shape, vt.dtype),
            pltpu.VMEM(dobs.shape, dobs.dtype),
            pltpu.SMEM(ranks.shape, ranks.dtype),
            pltpu.SemaphoreType.DMA((4,)),
            pltpu.SemaphoreType.DMA((blocks,)),
        ],
        cost_estimate=cost(5),
        compiler_params=packed,
    )(front, *held(y, maps, following, last), *far(cells, dinv, vt, dobs, ranks))

    wave, adj, image, token = pl.pallas_call(
        functools.partial(solve_kernel, fronts, rhs),
        name="solve",
        out_shape=(
            pltpu.VMEM((shots, rows), F32),
            pltpu.VMEM((shots, rows), F32),
            pltpu.VMEM((fronts * rhs, each, LANES), F32),
            pltpu.VMEM((8, LANES), F32),
        ),
        in_specs=[vmem] * 12,
        out_specs=[vmem] * 4,
        cost_estimate=cost(3),
        compiler_params=packed,
    )(*held(got, *fields))

    terms = lax.all_to_all(image, ("front", "rhs"), 0, 0)

    hit, pick = pl.pallas_call(
        functools.partial(table_kernel, fronts, slot),
        name="tables",
        out_shape=(
            pltpu.VMEM((MC_DEV // LANES, fronts * slot), BF16),
            pltpu.VMEM((LANES, fronts * slot), BF16),
        ),
        in_specs=[smem, vmem, vmem],
        out_specs=[vmem] * 2,
        cost_estimate=cost(4),
        compiler_params=room,
    )(front, *far(cells), *held(token))

    gradient = pl.pallas_call(
        functools.partial(gather_kernel, fronts, rhs),
        name="gather",
        out_shape=jax.ShapeDtypeStruct((MC_DEV // LANES, LANES), F32),
        in_specs=[vmem] * 3,
        out_specs=vmem,
        cost_estimate=cost(1),
        compiler_params=room,
    )(*held(terms, hit, pick))
    return (wave, adj, gradient.reshape(MC_DEV))


def solution(mesh):
    in_specs = (
        P("rhs", None),
        P(None, "front"),
        P("front", None, None),
        P("front", None, None),
        P("front", None, None),
        P("front"),
        P("rhs", "front"),
        P(),
    )
    out_specs = (P("rhs", "front"), P("rhs", "front"), P("front"))
    return jax.shard_map(body, mesh=mesh, in_specs=in_specs, out_specs=out_specs, check_vma=False)
```

```python
import functools

import jax
import jax.numpy as jnp
import numpy as np
from jax import lax
from jax.experimental import pallas as pl
from jax.experimental.pallas import tpu as pltpu
from jax.sharding import PartitionSpec as P

MC_DEV = 8192
LANES = 128
F32 = jnp.float32
BF16 = jnp.bfloat16
NN = (((1,), (0,)), ((), ()))
NT = (((1,), (1,)), ((), ()))


def dot(a, b, dims=NN):
    return lax.dot_general(a, b, dims, preferred_element_type=F32)


def parts(x):
    top = x.astype(BF16)
    return top, (x - top.astype(F32)).astype(BF16)


def dot3(a, b, dims=NN):
    rows = a[0].shape[0]
    first = dot(jnp.concatenate(a, axis=0), b[0], dims)
    return first[:rows] + first[rows:] + dot(a[0], b[1], dims)


def rows_of(pair, start, stop):
    return pair[0][start:stop], pair[1][start:stop]


def hits(count, index):
    return lax.broadcasted_iota(jnp.int32, (count, LANES), 0) == index


def as_ones(mask):
    return mask.astype(F32).astype(BF16)


def from_behind(array, axis, by):
    length = lax.axis_size(axis)
    return lax.ppermute(array, axis, [(i, (i + by) % length) for i in range(length)])


def prep_kernel(
    ranks_hbm, signs_hbm, sources_hbm, dinv_hbm, ut_hbm, vt_hbm, dobs_hbm,
    y_ref, maps_ref, back_ref,
    ranks_ref, signs_v, sources_v, dinv_v, ut_v, vt_v, dobs_v, small_sem, block_sem,
):
    blocks, rank_max, width = ut_v.shape
    shots = signs_v.shape[0]
    small = [
        pltpu.make_async_copy(signs_hbm, signs_v, small_sem.at[0]),
        pltpu.make_async_copy(ut_hbm, ut_v, small_sem.at[1]),
        pltpu.make_async_copy(vt_hbm, vt_v, small_sem.at[2]),
        pltpu.make_async_copy(dobs_hbm, dobs_v, small_sem.at[3]),
        pltpu.make_async_copy(ranks_hbm, ranks_ref, small_sem.at[4]),
    ]
    whole = [
        pltpu.make_async_copy(sources_hbm, sources_v, block_sem.at[0]),
        pltpu.make_async_copy(dinv_hbm, dinv_v, block_sem.at[1]),
    ]
    early = [small[0], whole[0]]
    late = small[1:] + [whole[1]]
    for copy in early + late:
        copy.start()
    for copy in early:
        copy.wait()

    sign = signs_v[...].astype(F32).astype(BF16)
    rank_row = lax.broadcasted_iota(jnp.int32, (rank_max, width), 0)
    products = {}
    for k in range(blocks):
        y_ref[k, :shots] = dot(sign, sources_v[:, k * width : (k + 1) * width])
    for copy in late:
        copy.wait()

    def sweep(k):
        left = jnp.where(rank_row < ranks_ref[k], ut_v[k], 0.0)
        y_ref[k] = dot3(parts(jnp.concatenate([y_ref[k, :shots], left], axis=0)), parts(dinv_v[k]), NT)

    def project(k):
        swept = y_ref[k]
        residual = parts(swept[:shots] - dobs_v[:, k * width : (k + 1) * width].astype(F32))
        swept = parts(swept)
        wave, ld = rows_of(swept, 0, shots), rows_of(swept, shots, None)
        if k + 1 < blocks:
            right = parts(jnp.where(rank_row < ranks_ref[k + 1], vt_v[k + 1], 0.0))
        else:
            right = parts(jnp.zeros((rank_max, width), F32))
        rows = tuple(jnp.concatenate(three, axis=0) for three in zip(wave, residual, ld))
        products[k] = dot3(rows, tuple(jnp.concatenate(two, axis=0) for two in zip(right, ld)), NT)

    for k in range(blocks):
        sweep(k)
    for k in range(blocks):
        project(k)

    n = rank_max
    nothing = jnp.zeros((n, n), F32)
    gains = [products[k][:shots, :n] for k in range(blocks)]
    fills = [products[k][shots : 2 * shots, n:] for k in range(blocks)]
    boths = [products[k][2 * shots :] for k in range(blocks)]

    def over(upper, product):
        return jnp.concatenate([upper - product[:shots], -product[shots:]], axis=0)

    joint = {}
    for k in range(1, blocks - 2, 2):
        follow = jnp.concatenate([gains[k], -boths[k][:, :n]], axis=0)
        joint[k] = over(gains[k + 1], dot3(parts(follow), parts(boths[k + 1][:, :n])))
    states = [None] * blocks
    states[1] = jnp.concatenate([gains[0], -boths[0][:, :n]], axis=0)
    pushes = [jnp.concatenate([fills[0], -boths[0][:, n:]], axis=0)] + [None] * (blocks - 1)
    for k in range(1, blocks):
        weights = [boths[k]]
        if k in joint:
            weights.append(-joint[k][shots:])
        after = dot3(parts(states[k]), parts(jnp.concatenate(weights, axis=1)))
        pushes[k] = over(fills[k], after[:, n : 2 * n])
        if k % 2 and k + 1 < blocks:
            states[k + 1] = over(gains[k], after[:, :n])
        if k in joint:
            states[k + 2] = over(joint[k][:shots], after[:, 2 * n :])
    long = jnp.concatenate(pushes[1:], axis=1)
    back = pushes[0] + dot3(parts(long), parts(jnp.concatenate([state[shots:] for state in states[1:]], axis=1)), NT)
    for k in range(blocks):
        if k + 1 < blocks:
            maps_ref[k, :, :n] = states[k + 1]
        maps_ref[k, :, n : 2 * n] = pushes[k]
        maps_ref[k, :n, 2 * n :] = boths[k]
    back_ref[...] = back


def send_kernel(fronts, y_ref, maps_ref, next_ref, back_ref, send_ref, last_ref):
    blocks = y_ref.shape[0]
    shots = y_ref.shape[1] - next_ref.shape[0]
    passed = dot3(parts(y_ref[blocks - 1]), parts(next_ref[...]), NT)
    forward = -passed[shots:]
    last_ref[...] = forward
    state = dot3(parts(maps_ref[blocks - 2, :, : forward.shape[0]]), parts(forward))
    back = back_ref[...]
    payload = jnp.concatenate(
        [state[shots:], state[:shots] + passed[:shots], back[shots:], back[:shots]], axis=1
    )
    for g in range(fronts):
        send_ref[g] = payload


def fields_kernel(
    fronts, slot, front_ref, y_ref, maps_ref, next_ref, last_ref, map_hbm, dinv_hbm, vt_hbm, dobs_hbm, ranks_hbm,
    wave_ref, wave_top, wave_rest, adj_ref, ahead_top, ahead_rest, behind_top, behind_rest, hit_ref, pick_ref, mine_ref,
    map_v, dinv_v, vt_v, dobs_v, ranks_ref, sem, block_sem,
):
    blocks, n, width = vt_v.shape
    shots = dobs_v.shape[0]
    groups = map_v.shape[0]
    start = pl.multiple_of(front_ref[0] * groups, groups)
    mine_ref[...] = (lax.broadcasted_iota(jnp.int32, mine_ref.shape, 0) == front_ref[0]).astype(F32)
    fetch = [
        pltpu.make_async_copy(vt_hbm, vt_v, sem.at[0]),
        pltpu.make_async_copy(dobs_hbm, dobs_v, sem.at[1]),
        pltpu.make_async_copy(ranks_hbm, ranks_ref, sem.at[2]),
        pltpu.make_async_copy(map_hbm.at[pl.ds(start, groups)], map_v, sem.at[3]),
    ]
    for copy in fetch:
        copy.start()
    large = [pltpu.make_async_copy(dinv_hbm.at[k], dinv_v.at[k], block_sem.at[k]) for k in range(blocks)]
    for copy in large:
        copy.start()

    unit_row = lax.broadcasted_iota(jnp.int32, (n, n), 0)
    unit_lane = lax.broadcasted_iota(jnp.int32, (n, n), 1)
    unit = (unit_row == unit_lane).astype(F32)
    nothing = jnp.zeros((n, n), F32)
    state = jnp.concatenate([jnp.zeros((shots + n, n), F32), unit], axis=0)
    backs = [None] * blocks
    for k in range(blocks - 1, 0, -1):
        backs[k] = state
        factor = parts(last_ref[...] if k + 1 == blocks else -maps_ref[k, :n, 2 * n : 3 * n])
        state = dot3(parts(state), factor, NT) + jnp.concatenate([maps_ref[k, :, n : 2 * n], nothing], axis=0)
    backs[0] = state
    for copy in fetch:
        copy.wait()

    owner = map_v[...] >> (MC_DEV.bit_length() - 1)
    member = jnp.concatenate([hits(fronts, owner[j : j + 1]).astype(F32) for j in range(groups)], axis=0)
    ranked = member * rank_in_order(member, fronts, groups, False)
    place = jnp.concatenate(
        [jnp.sum(ranked[j * fronts : (j + 1) * fronts], axis=0, keepdims=True) for j in range(groups)], axis=0
    ).astype(jnp.int32) + owner * slot
    out_rows = hit_ref.shape[0]
    for j in range(groups):
        lanes = slice(j * LANES, (j + 1) * LANES)
        at = place[j : j + 1]
        hit_ref[:, lanes] = as_ones(hits(out_rows, at >> 7))
        pick_ref[:, lanes] = as_ones(hits(LANES, at & (LANES - 1)))

    for copy in large:
        copy.wait()
    rank_row = lax.broadcasted_iota(jnp.int32, (n, width), 0)

    for k in range(blocks):
        columns = slice(k * width, (k + 1) * width)
        if k + 1 < blocks:
            right = jnp.where(rank_row < ranks_ref[k + 1], vt_v[k + 1], 0.0)
        else:
            right = next_ref[...]
        residual = y_ref[k, :shots] - dobs_v[:, columns].astype(F32)
        rows = jnp.concatenate([residual, y_ref[k, shots:], right], axis=0)
        returned = dot3(parts(rows), parts(dinv_v[k]))
        if k > 0:
            ahead = maps_ref[k - 1, :, :n]
        else:
            ahead = jnp.concatenate([jnp.zeros((shots, n), F32), unit], axis=0)
        wave = dot3(parts(ahead), parts(y_ref[k, shots:]))
        wave_ref[:, columns] = y_ref[k, :shots] - wave[:shots]
        wave_top[:, columns], wave_rest[:, columns] = parts(-wave[shots:])
        enters = jnp.concatenate([jnp.concatenate([ahead, nothing], axis=0), backs[k]], axis=1)
        adj = dot3(parts(enters), parts(returned[shots:]))
        adj_ref[:, columns] = returned[:shots] - adj[:shots]
        ahead_top[:, columns], ahead_rest[:, columns] = parts(-adj[shots : shots + n])
        behind_top[:, columns], behind_rest[:, columns] = parts(-adj[shots + n :])


def rank_in_order(member, stride, groups, blocked):
    count = member.shape[0]
    row = lax.broadcasted_iota(jnp.int32, (LANES, LANES), 0)
    lane = lax.broadcasted_iota(jnp.int32, (LANES, LANES), 1)
    member = member.astype(BF16)
    inside = dot(member, as_ones(row < lane))
    total = dot(member, jnp.ones((LANES, LANES), BF16))
    p = lax.broadcasted_iota(jnp.int32, (count, count), 0)
    q = lax.broadcasted_iota(jnp.int32, (count, count), 1)
    if blocked:
        shift = groups.bit_length() - 1
        same = (p >> shift) == (q >> shift)
    else:
        same = (p & (stride - 1)) == (q & (stride - 1))
    return inside + dot(as_ones(same & (q < p)), total.astype(BF16))


def solve_kernel(
    fronts, rhs, got_ref, wave_ref, wave_top, wave_rest, adj_ref, ahead_top, ahead_rest,
    behind_top, behind_rest, hit_ref, pick_ref, mine_ref,
    wave_out, adj_out, image_out, token_ref,
):
    shots, rows = wave_ref.shape
    n = wave_top.shape[0]
    token_ref[...] = jnp.zeros_like(token_ref)
    ahead_v, behind_v = {}, {}
    zero = jnp.zeros((shots, n), F32)

    maps = [parts(got_ref[g, :, :n]) for g in range(fronts)]
    gains = [got_ref[g, :, n : 2 * n] for g in range(fronts)]
    joint = {g: parts(dot3(maps[g], maps[g + 1])) for g in range(1, fronts - 1, 2)}
    ahead_v[0] = zero
    ahead_v[1] = gains[0]
    state = gains[0]
    pushes = [None] * fronts

    def push(g, pair):
        pushes[g] = dot3(pair, parts(got_ref[g, :, 2 * n : 3 * n])) + got_ref[g, :, 3 * n :]

    for g in range(1, fronts - 1, 2):
        pair = parts(state)
        state = dot3(pair, joint[g]) + (dot3(parts(gains[g]), maps[g + 1]) + gains[g + 1])
        push(g, pair)
        between = dot3(pair, maps[g]) + gains[g]
        ahead_v[g + 1] = between
        push(g + 1, parts(between))
        ahead_v[g + 2] = state
    push(fronts - 1, parts(state))
    behind_v[fronts - 1] = zero
    state = pushes[fronts - 1]
    behind_v[fronts - 2] = state
    for g in range(fronts - 3, 0, -2):
        pair = parts(state)
        state = dot3(pair, joint[g], NT) + (dot3(parts(pushes[g + 1]), maps[g], NT) + pushes[g])
        behind_v[g] = dot3(pair, maps[g + 1], NT) + pushes[g + 1]
        behind_v[g - 1] = state

    def own(choices):
        value = choices[0]
        for g in range(1, fronts):
            value = jnp.where(mine_ref[g : g + 1, :n] > 0.5, choices[g], value)
        return parts(value)

    ahead = own(ahead_v)
    wave = wave_ref[...] + dot3(ahead, (wave_top[...], wave_rest[...]))
    wave_out[...] = wave
    adj = adj_ref[...] + dot3(ahead, (ahead_top[...], ahead_rest[...]))
    adj = adj + dot3(own(behind_v), (behind_top[...], behind_rest[...]))
    adj_out[...] = adj
    image = jnp.sum(wave * adj, axis=0, keepdims=True) * (1.0 / (shots * rhs))
    top, rest = parts(image)
    hit = hit_ref[...]
    out_rows = hit.shape[0]
    table = jnp.concatenate([hit * top, hit * rest], axis=0)
    packed = dot(table, pick_ref[...], NT)
    packed = packed[:out_rows] + packed[out_rows:]
    each = out_rows // fronts
    for g in range(fronts):
        for r in range(rhs):
            image_out[g * rhs + r] = packed[g * each : (g + 1) * each]


def table_kernel(fronts, slot, front_ref, map_ref, token_ref, hit_ref, pick_ref):
    del token_ref
    each = slot // LANES
    count = map_ref.shape[0]
    groups = count // fronts
    cells = map_ref[...]
    mine = (cells >> (MC_DEV.bit_length() - 1)) == front_ref[0]
    rank = rank_in_order(mine.astype(F32), fronts, groups, True).astype(jnp.int32)
    rank = jnp.where(mine, rank, -1)
    local = cells & (MC_DEV - 1)
    coarse = (local >> 7).astype(F32)
    fine = (local & (LANES - 1)).astype(F32)
    high = rank >> 7
    low = jnp.where(mine, rank & (LANES - 1), -1)
    for f in range(fronts):
        table, pick = [], []
        for j in range(f * groups, (f + 1) * groups):
            hit = hits(each, high[j : j + 1])
            table.append(
                jnp.concatenate(
                    [jnp.where(hit, coarse[j : j + 1], 0.0), jnp.where(hit, fine[j : j + 1], 0.0)], axis=0
                ).astype(BF16)
            )
            pick.append(as_ones(hits(LANES, low[j : j + 1])))
        found = dot(jnp.concatenate(table, axis=1), jnp.concatenate(pick, axis=1), NT).astype(jnp.int32)
        for j in range(each):
            lanes = slice((f * each + j) * LANES, (f * each + j + 1) * LANES)
            hit_ref[:, lanes] = as_ones(hits(MC_DEV // LANES, found[j : j + 1]))
            pick_ref[:, lanes] = as_ones(hits(LANES, found[each + j : each + j + 1]))


def gather_kernel(fronts, rhs, terms_ref, hit_ref, pick_ref, out_ref):
    each = terms_ref.shape[1]
    rows = []
    for g in range(fronts):
        terms = terms_ref[g * rhs]
        for r in range(1, rhs):
            terms = terms + terms_ref[g * rhs + r]
        rows += [terms[j : j + 1] for j in range(each)]
    top, rest = parts(jnp.concatenate(rows, axis=1))
    hit = hit_ref[...]
    out_rows = hit.shape[0]
    found = dot(jnp.concatenate([hit * top, hit * rest], axis=0), pick_ref[...], NT)
    out_ref[...] = found[:out_rows] + found[out_rows:]


def body(signs, sources, dinv, u_fac, v_fac, ranks, dobs, cellmap):
    shots = signs.shape[0]
    blocks, width, n = u_fac.shape
    rows = blocks * width
    fronts = lax.axis_size("front")
    rhs = lax.axis_size("rhs")
    cap = 2 * rows // fronts
    slot = (cap + LANES - 1) // LANES * LANES
    each = slot // LANES
    groups = rows // LANES
    front = lax.axis_index("front").astype(jnp.int32).reshape(1)
    ut = jnp.swapaxes(u_fac, 1, 2)
    vt = jnp.swapaxes(v_fac, 1, 2)
    cells = cellmap.reshape(-1, LANES)
    middle = np.repeat(np.arange(n, dtype=np.float32)[:, None] + 0.5, width, axis=1)
    alive = jnp.where(lax.axis_index("front") == 0, 0, ranks[0]).astype(F32)
    following = from_behind(jnp.where(middle < alive, vt[0], 0.0), "front", -1)

    smem = pl.BlockSpec(memory_space=pltpu.SMEM)
    vmem = pl.BlockSpec(memory_space=pltpu.VMEM)
    hbm = pl.BlockSpec(memory_space=pltpu.HBM)

    def held(*arrays):
        return [pltpu.with_memory_space_constraint(a, pltpu.VMEM) for a in arrays]

    def far(*arrays):
        return [pltpu.with_memory_space_constraint(a, pltpu.HBM) for a in arrays]

    def cost(us):
        return pl.CostEstimate(flops=int(us * 1e9), bytes_accessed=int(us * 3e6), transcendentals=0)

    room = pltpu.CompilerParams(vmem_limit_bytes=24 * 2**20)
    packed = pltpu.CompilerParams(vmem_limit_bytes=24 * 2**20)

    y, maps, back = pl.pallas_call(
        prep_kernel,
        name="prep",
        out_shape=(
            pltpu.VMEM((blocks, shots + n, width), F32),
            pltpu.VMEM((blocks, shots + n, 4 * n), F32),
            pltpu.VMEM((shots + n, n), F32),
        ),
        in_specs=[hbm] * 7,
        out_specs=[vmem] * 3,
        scratch_shapes=[
            pltpu.SMEM(ranks.shape, ranks.dtype),
            pltpu.VMEM(signs.shape, signs.dtype),
            pltpu.VMEM(sources.shape, sources.dtype),
            pltpu.VMEM(dinv.shape, dinv.dtype),
            pltpu.VMEM(ut.shape, ut.dtype),
            pltpu.VMEM(vt.shape, vt.dtype),
            pltpu.VMEM(dobs.shape, dobs.dtype),
            pltpu.SemaphoreType.DMA((5,)),
            pltpu.SemaphoreType.DMA((2,)),
        ],
        cost_estimate=cost(6),
        compiler_params=packed,
    )(*far(ranks, signs, sources, dinv, ut, vt, dobs))

    send, last = pl.pallas_call(
        functools.partial(send_kernel, fronts),
        name="send",
        out_shape=(pltpu.VMEM((fronts, n, 4 * n), F32), pltpu.VMEM((n, n), F32)),
        in_specs=[vmem] * 4,
        out_specs=[vmem] * 2,
        cost_estimate=cost(0.5),
            )(*held(y, maps, following, back))

    got = lax.all_to_all(send, "front", 0, 0)

    fields = pl.pallas_call(
        functools.partial(fields_kernel, fronts, slot),
        name="fields",
        out_shape=(
            pltpu.VMEM((shots, rows), F32),
            pltpu.VMEM((n, rows), BF16),
            pltpu.VMEM((n, rows), BF16),
            pltpu.VMEM((shots, rows), F32),
            pltpu.VMEM((n, rows), BF16),
            pltpu.VMEM((n, rows), BF16),
            pltpu.VMEM((n, rows), BF16),
            pltpu.VMEM((n, rows), BF16),
            pltpu.VMEM((fronts * each, rows), BF16),
            pltpu.VMEM((LANES, rows), BF16),
            pltpu.VMEM((fronts, LANES), F32),
        ),
        in_specs=[smem] + [vmem] * 4 + [hbm] * 5,
        out_specs=[vmem] * 11,
        scratch_shapes=[
            pltpu.VMEM((groups, LANES), cells.dtype),
            pltpu.VMEM(dinv.shape, dinv.dtype),
            pltpu.VMEM(vt.shape, vt.dtype),
            pltpu.VMEM(dobs.shape, dobs.dtype),
            pltpu.SMEM(ranks.shape, ranks.dtype),
            pltpu.SemaphoreType.DMA((4,)),
            pltpu.SemaphoreType.DMA((blocks,)),
        ],
        cost_estimate=cost(5),
        compiler_params=packed,
    )(front, *held(y, maps, following, last), *far(cells, dinv, vt, dobs, ranks))

    wave, adj, image, token = pl.pallas_call(
        functools.partial(solve_kernel, fronts, rhs),
        name="solve",
        out_shape=(
            pltpu.VMEM((shots, rows), F32),
            pltpu.VMEM((shots, rows), F32),
            pltpu.VMEM((fronts * rhs, each, LANES), F32),
            pltpu.VMEM((8, LANES), F32),
        ),
        in_specs=[vmem] * 12,
        out_specs=[vmem] * 4,
        cost_estimate=cost(3),
        compiler_params=packed,
    )(*held(got, *fields))

    terms = lax.all_to_all(image, ("front", "rhs"), 0, 0)

    hit, pick = pl.pallas_call(
        functools.partial(table_kernel, fronts, slot),
        name="tables",
        out_shape=(
            pltpu.VMEM((MC_DEV // LANES, fronts * slot), BF16),
            pltpu.VMEM((LANES, fronts * slot), BF16),
        ),
        in_specs=[smem, vmem, vmem],
        out_specs=[vmem] * 2,
        cost_estimate=cost(4),
        compiler_params=room,
    )(front, *far(cells), *held(token))

    gradient = pl.pallas_call(
        functools.partial(gather_kernel, fronts, rhs),
        name="gather",
        out_shape=jax.ShapeDtypeStruct((MC_DEV // LANES, LANES), F32),
        in_specs=[vmem] * 3,
        out_specs=vmem,
        cost_estimate=cost(1),
        compiler_params=room,
    )(*held(terms, hit, pick))
    return (wave, adj, gradient.reshape(MC_DEV))


def solution(mesh):
    in_specs = (
        P("rhs", None),
        P(None, "front"),
        P("front", None, None),
        P("front", None, None),
        P("front", None, None),
        P("front"),
        P("rhs", "front"),
        P(),
    )
    out_specs = (P("rhs", "front"), P("rhs", "front"), P("front"))
    return jax.shard_map(body, mesh=mesh, in_specs=in_specs, out_specs=out_specs, check_vma=False)
```
